256 devices in a mesh: attn: 32 (over y, z), proj: 8 (over x, core).
Axes of the slice: x: 4, y: 4, z: 8, core: 2. Of those that a mesh axis runs over, the one named last changes fastest.
Arguments:
- tokens: bfloat16 [16384, 4096], P('attn', 'proj'), may hold values from -6 to 6
- norm_gain: float32 [4096], replicated, may hold values from 0.1 to 1.9
- w_query: bfloat16 [4096, 4096], P(None, 'proj')
- w_key: bfloat16 [4096, 1024], P(None, 'proj')
- value_matrix: bfloat16 [4096, 1024], P(None, 'proj'), may hold values from -0.09375 to 0.09375
- doc_lengths: int32 [128], replicated, may hold values from 1 to 512, 16384 in all
- block_server: int32 [128], P('attn'), may hold values from 0 to 31, as said below
Outputs:
- attn_out: bfloat16 [16384, 4096], P('attn', 'proj')
- served_lse: float32 [128, 32, 128], P('attn', 'proj')
The draws below stay inside these ranges and needn't reach their ends.
Inputs may be any that keep to these rules, and one draw needn't show every extreme that they name: `doc_lengths`: the lengths sum to 16384. `block_server`: query block b belongs to the micro-batch b // 4; every index of attn serves exactly 4 blocks, and at most one block of any one micro-batch.
All inputs are finite; a program needn't handle non-finite values.
Results may differ from the reference program's by a relative error of at most 0.0074.
Values may be sent and summed in bfloat16 or wider, within the bound.
A program may use at most 128 MiB of HBM per device.

```python
import math
import jax
import jax.numpy as jnp
import numpy as np
from jax import lax

MODEL_DIMENSION = 4096
QUERY_HEADS = 32
KEY_VALUE_HEADS = 8
HEAD_SIZE = 128
QUERY_BLOCK_ROWS = 128
BPS = 4
TOKENS = 16384
NB = 128
MAXDOC = 512
NDOCS = 128
HEADS_PER_GROUP = 4
N_ATTN = 32


def draw_tokens(key, part):
    starting_row = jax.random.normal(jax.random.fold_in(key, 22), (TOKENS, MODEL_DIMENSION), jnp.float32)
    return jnp.clip(starting_row, -6.0, 6.0).astype(jnp.bfloat16)


def grouped_keys(key):
    return jax.random.normal(jax.random.fold_in(key, 31), (MODEL_DIMENSION, KEY_VALUE_HEADS * HEAD_SIZE), jnp.float32) / MODEL_DIMENSION ** 0.5


def draw_w_key(key, part):
    return grouped_keys(key).astype(jnp.bfloat16)


def draw_w_query(key, part):
    own = jax.random.normal(jax.random.fold_in(key, 32), (MODEL_DIMENSION, QUERY_HEADS * HEAD_SIZE), jnp.float32) / MODEL_DIMENSION ** 0.5
    return own.astype(jnp.bfloat16)


def draw_block_server(key, part):
    sigma = jax.random.permutation(jax.random.fold_in(key, 41), N_ATTN)
    tau = jax.random.permutation(jax.random.fold_in(key, 42), N_ATTN)
    offsets = jax.random.permutation(jax.random.fold_in(key, 43), N_ATTN)[:BPS]
    blocks = jnp.arange(NB, dtype=jnp.int32)
    owner = blocks // BPS
    within = blocks % BPS
    return sigma[(tau[owner] + offsets[within]) % N_ATTN].astype(jnp.int32)


def shard_levels(own_key, shape, split, least, largest):
    gain, own = 1.0, jax.random.fold_in(own_key, 6)
    for position, blocks in split:
        heights = jnp.exp(jax.random.uniform(jax.random.fold_in(own, position), (blocks,), jnp.float32, least / len(split), largest / len(split)))
        gain = gain * jnp.repeat(heights, shape[position] // blocks).reshape([-1 if axis == position else 1 for axis in range(len(shape))])
    return gain


def length_profile(count, total, reach, slope):
    loads = [(1 << 20) // math.isqrt(grade ** slope) + 1 for grade in range(2, count + 1)]
    surplus, counts = total - reach - (count - 1), [1] * (count - 1)
    while surplus > 0:
        candidates = [i for i in range(count - 1) if counts[i] < reach]
        pool, remaining = sum([loads[i] for i in candidates]), surplus
        for i in candidates:
            more = min(reach - counts[i], max(1, remaining * loads[i] // pool), surplus)
            counts[i] = counts[i] + more
            surplus = surplus - more
    return np.array([reach] + counts)


def uneven_parts(rng, number_of, total, bound, skew):
    if number_of == 2:
        one = jax.random.randint(rng, (), max(1, total - bound), min(bound, total - 1) + 1)
        return jnp.stack([one, total - one])
    lengths = jnp.asarray(length_profile(number_of, total, bound, skew), jnp.int32)
    pairs = (number_of - 1) // 2
    donor, sink = lengths[1:1 + 2 * pairs:2], lengths[2:2 + 2 * pairs:2]
    margin = jnp.minimum(donor - 1, bound - sink)
    passed = jax.random.randint(jax.random.fold_in(rng, 1), (pairs,), 0, 1 << 20) % (margin + 1)
    lengths = lengths.at[1:1 + 2 * pairs:2].set(donor - passed).at[2:2 + 2 * pairs:2].set(sink + passed)
    return lengths[jax.random.permutation(jax.random.fold_in(rng, 2), number_of)]


def scatter_about(key, extent, spread, bound, pieces=(), held_as=jnp.bfloat16):
    loudness = shard_levels(key, extent, pieces, -0.22, 0.18) if pieces else 1.0
    values = jax.random.normal(key, extent, jnp.float32) * spread * loudness
    return jnp.minimum(jnp.maximum(values, -bound), bound).astype(held_as)


def setup_inputs(seed: int = 0) -> dict:
    splits = jax.random.split(jax.random.key(seed), 8)
    tokens = draw_tokens(jax.random.fold_in(splits[7], 71), 0)
    norm_gain = jnp.clip(1.0 + 0.18 * jax.random.normal(splits[1], (MODEL_DIMENSION,), jnp.float32), 0.1, 1.9)
    w_query = draw_w_query(jax.random.fold_in(splits[7], 71), 0)
    w_key = draw_w_key(jax.random.fold_in(splits[7], 71), 0)
    value_matrix = scatter_about(splits[4], (MODEL_DIMENSION, KEY_VALUE_HEADS * HEAD_SIZE), MODEL_DIMENSION ** -0.5, 0.09375, ((1, 8),))
    doc_lengths = uneven_parts(splits[5], NDOCS, TOKENS, MAXDOC, 2).astype(jnp.int32)
    block_server = draw_block_server(jax.random.fold_in(splits[7], 71), 0)
    return dict(tokens=tokens, norm_gain=norm_gain, w_query=w_query, w_key=w_key, value_matrix=value_matrix, doc_lengths=doc_lengths, block_server=block_server)


big_value = 1e+30
norm_eps = 1e-05

def reference(tokens, norm_gain, w_query, w_key, value_matrix, doc_lengths, block_server):
    inputs = tokens.astype(jnp.float32)
    inverse = lax.rsqrt(lax.optimization_barrier(jnp.sum(inputs * inputs, axis=1, keepdims=True)) / MODEL_DIMENSION + norm_eps)
    scaled = (inputs * norm_gain).astype(jnp.bfloat16)
    query_vectors = (jnp.dot(scaled, w_query, preferred_element_type=jnp.float32) * inverse).astype(jnp.bfloat16)
    keys = (jnp.dot(scaled, w_key, preferred_element_type=jnp.float32) * inverse).astype(jnp.bfloat16)
    values = (jnp.dot(scaled, value_matrix, preferred_element_type=jnp.float32) * inverse).astype(jnp.bfloat16)
    ends = jnp.cumsum(doc_lengths).astype(jnp.int32)
    starts = (ends - doc_lengths).astype(jnp.int32)
    positions = jnp.arange(TOKENS, dtype=jnp.int32)
    first = lax.optimization_barrier(jnp.max(jnp.where(starts[None, :] <= positions[:, None], starts[None, :], 0), axis=1)).astype(jnp.int32)
    padded_keys = jnp.pad(keys, ((MAXDOC, 0), (0, 0)))
    padded_values = jnp.pad(values, ((MAXDOC, 0), (0, 0)))
    row_extent = MAXDOC + QUERY_BLOCK_ROWS
    scale = 1.0 / HEAD_SIZE ** 0.5

    def one_block(block):
        starting_row = (block * QUERY_BLOCK_ROWS).astype(jnp.int32)
        query_row_block = lax.dynamic_slice_in_dim(query_vectors, starting_row, QUERY_BLOCK_ROWS, 0).astype(jnp.float32).reshape(QUERY_BLOCK_ROWS, KEY_VALUE_HEADS, HEADS_PER_GROUP, HEAD_SIZE)
        key_matrix_rows = lax.dynamic_slice_in_dim(padded_keys, starting_row, row_extent, 0).astype(jnp.float32).reshape(row_extent, KEY_VALUE_HEADS, HEAD_SIZE)
        value_matrix_rows = lax.dynamic_slice_in_dim(padded_values, starting_row, row_extent, 0).astype(jnp.float32).reshape(row_extent, KEY_VALUE_HEADS, HEAD_SIZE)
        key_pos = starting_row - MAXDOC + jnp.arange(row_extent, dtype=jnp.int32)
        query_pos = starting_row + jnp.arange(QUERY_BLOCK_ROWS, dtype=jnp.int32)
        row_first = lax.dynamic_slice_in_dim(first, starting_row, QUERY_BLOCK_ROWS, 0)
        allowed = (key_pos[None, :] >= row_first[:, None]) & (key_pos[None, :] <= query_pos[:, None])
        scores = jnp.einsum('qngd,knd->ngqk', query_row_block, key_matrix_rows) * scale
        scores = jnp.where(allowed, scores, -big_value)
        highest = lax.optimization_barrier(jnp.max(scores, axis=-1))
        weights = jnp.where(allowed, jnp.exp(scores - highest[..., None]), 0.0)
        total = lax.optimization_barrier(jnp.sum(weights, axis=-1))
        rounded = lax.optimization_barrier(weights.astype(jnp.bfloat16))
        summed = jnp.einsum('ngqk,knd->ngqd', rounded.astype(jnp.float32), value_matrix_rows)
        result = summed / total[..., None]
        result = jnp.transpose(result, (2, 0, 1, 3)).reshape(QUERY_BLOCK_ROWS, QUERY_HEADS * HEAD_SIZE).astype(jnp.bfloat16)
        lse = (highest + jnp.log(total)).reshape(QUERY_HEADS, QUERY_BLOCK_ROWS)
        return (result, lse)
    results, lses = lax.map(one_block, jnp.arange(NB, dtype=jnp.int32))
    attn_out = results.reshape(TOKENS, QUERY_HEADS * HEAD_SIZE)
    order = jnp.argsort(block_server * NB + jnp.arange(NB, dtype=jnp.int32), stable=True)
    served_lse = lses[order]
    return (attn_out, served_lse)
```

```python
import jax
import jax.numpy as jnp
from jax import lax
from jax.sharding import PartitionSpec as P

HEAD = 128
QB = 128
NEG = -1e30
norm_eps = 1e-05


def shards(tokens, norm_gain, w_query, w_key, value_matrix, doc_lengths, block_server):
    rows = tokens.shape[0]
    model_width = w_query.shape[0]
    heads = w_query.shape[1] // HEAD
    blocks = rows // QB
    servers = lax.axis_size("attn")
    me = lax.axis_index("attn")
    wide = lax.all_gather(tokens, "proj", axis=1, tiled=True).astype(jnp.float32)
    scaled = (wide * norm_gain[None, :]).astype(jnp.bfloat16)
    squares = jnp.sum(wide * wide, axis=1, keepdims=True)
    inverse = lax.rsqrt(squares / model_width + norm_eps)
    dot = lambda w: (jnp.dot(scaled, w, preferred_element_type=jnp.float32) * inverse).astype(jnp.bfloat16)
    k = dot(w_key)
    v = dot(value_matrix)
    kv = jnp.concatenate([k, v], axis=1)
    prior = lax.ppermute(kv, "attn", [(i, (i + 1) % servers) for i in range(servers)])
    q = dot(w_query)
    allkv = jnp.concatenate([prior, kv], axis=0)
    starts = jnp.cumsum(doc_lengths) - doc_lengths
    extent = rows + QB
    outs, lses = [], []
    for b in range(blocks):
        pos = me * rows + b * QB + jnp.arange(QB, dtype=jnp.int32)
        first = jnp.max(jnp.where(starts[None, :] <= pos[:, None], starts[None, :], 0), axis=1)
        kpos = (me - 1) * rows + b * QB + jnp.arange(extent, dtype=jnp.int32)
        allowed = (kpos[None, :] >= first[:, None]) & (kpos[None, :] <= pos[:, None])
        win = allkv[b * QB:b * QB + extent]
        qb = q[b * QB:(b + 1) * QB].reshape(QB, heads, HEAD)
        s = jnp.einsum("qhd,kd->hqk", qb, win[:, :HEAD], preferred_element_type=jnp.float32)
        s = jnp.where(allowed, s * (1.0 / HEAD ** 0.5), NEG)
        m = jnp.max(s, axis=-1)
        w = jnp.where(allowed, jnp.exp(s - m[..., None]), 0.0)
        total = jnp.sum(w, axis=-1)
        o = jnp.einsum("hqk,kd->hqd", w.astype(jnp.bfloat16), win[:, HEAD:], preferred_element_type=jnp.float32)
        o = (o / total[..., None]).transpose(1, 0, 2).reshape(QB, heads * HEAD).astype(jnp.bfloat16)
        outs.append(o)
        lses.append(m + jnp.log(total))
    attn_out = jnp.concatenate(outs, axis=0)
    lse = jnp.stack(lses)
    slot = jnp.arange(servers, dtype=jnp.int32)
    sending = block_server[None, :] == slot[:, None]
    send = jnp.sum(jnp.where(sending[:, :, None, None], lse[None], 0.0), axis=1)
    flag = jnp.any(sending, axis=1).astype(jnp.float32)
    send = jnp.concatenate([send, jnp.broadcast_to(flag[:, None, None], (servers, 1, QB))], axis=1)
    recv = lax.all_to_all(send, "attn", split_axis=0, concat_axis=0, tiled=True)
    valid = recv[:, heads, 0] > 0
    rank = jnp.cumsum(valid.astype(jnp.int32)) - 1
    pick = (rank[None, :] == jnp.arange(blocks, dtype=jnp.int32)[:, None]) & valid[None, :]
    served = jnp.sum(jnp.where(pick[:, :, None, None], recv[None, :, :heads], 0.0), axis=1)
    return attn_out, served


def solution(mesh):
    return jax.shard_map(
        shards,
        mesh=mesh,
        in_specs=(
            P("attn", "proj"),
            P(),
            P(None, "proj"),
            P(None, "proj"),
            P(None, "proj"),
            P(),
            P("attn"),
        ),
        out_specs=(P("attn", "proj"), P("attn", "proj", None)),
        check_vma=False,
    )
```

```python
import functools
import jax
import jax.numpy as jnp
from jax import lax
from jax.experimental import pallas as pl
from jax.experimental.pallas import tpu as pltpu
from jax.sharding import PartitionSpec as P

HEAD = 128
QB = 128
NEG = -1e30
EPS = 1e-05
LOG2E = 1.4426950408889634
LN2 = 0.6931471805599453
MESH = pl.DeviceIdType.MESH
NC = 4


def fused(n_attn, nz, tok, gain_h, wq, wk, wv, lens_h, served_h, out, lse_out,
          gain, lens, served, X, W, XS, G, KV, PKV, Q, FR, M, L, ACC, SLOT, RECV, PART,
          own_sem, in_sem, w_sem, s_sem, r_sem, kvs_sem, kvr_sem, ls_sem, lr_sem):
    f32 = jnp.float32
    bf16 = jnp.bfloat16
    a = lax.axis_index("attn")
    p = lax.axis_index("proj")
    core = lax.rem(p, 2)
    s = 1 - 2 * core
    mod8 = lambda v: lax.rem(v + 16, 8)
    partner = p + s
    ahead = mod8(p + 2 * s)
    behind = mod8(p - 2 * s)
    kinds = [p, partner, behind, ahead, mod8(p + 3 * s), mod8(p - s), mod8(p + 4), mod8(p + s + 4)]
    ny = n_attn // nz
    y = a // nz
    z = lax.rem(a, nz)
    offs = [(dy, dz) for dy in range(ny) for dz in range(nz) if (dy, dz) != (0, 0)]
    offs.sort(key=lambda o: -(min(o[0], ny - o[0]) + min(o[1], nz - o[1])))
    peers = [lax.rem(y + dy, ny) * nz + lax.rem(z + dz, nz) for dy, dz in offs]
    nxt = lax.rem(a + 1, n_attn)

    for t, k in enumerate(kinds):
        r = pl.ds(pl.multiple_of(k * 512, 512), 512)
        d = pl.ds(t * 512, 512)
        pltpu.make_async_copy(wq.at[r, :], W.at[d, pl.ds(0, 512)], w_sem.at[t, 0]).start()
        pltpu.make_async_copy(wk.at[r, :], W.at[d, pl.ds(512, 128)], w_sem.at[t, 1]).start()
        pltpu.make_async_copy(wv.at[r, :], W.at[d, pl.ds(640, 128)], w_sem.at[t, 2]).start()
    own_copy = pltpu.make_async_copy(tok, X.at[0], own_sem)
    own_copy.start()
    small = [pltpu.make_async_copy(src, dst, in_sem.at[i])
             for i, (src, dst) in enumerate(((gain_h, gain), (lens_h, lens), (served_h, served)))]
    for cp in small:
        cp.start()

    barrier = pltpu.get_barrier_semaphore()
    for d in (ahead, behind, partner):
        pl.semaphore_signal(barrier, inc=1, device_id=(a, d), device_id_type=MESH)
    for d in peers:
        pl.semaphore_signal(barrier, inc=1, device_id=(d, p), device_id_type=MESH)
    pl.semaphore_wait(barrier, 3 + len(peers))

    def rows(c):
        return pl.ds((NC - 1 - c) * QB, QB)

    def rc(c, kind, src, dst_proj):
        return pltpu.make_async_remote_copy(
            src_ref=src, dst_ref=X.at[kind, rows(c), :],
            send_sem=s_sem.at[c, kind], recv_sem=r_sem.at[c, kind],
            device_id=(a, dst_proj), device_id_type=MESH)

    def send_own(c):
        src = tok.at[rows(c), :]
        rc(c, 2, src, ahead).start()
        rc(c, 3, src, behind).start()
        rc(c, 1, src, partner).start()

    def recv(c, kind):
        rc(c, kind, X.at[kind, rows(c), :], partner).wait_recv()

    def relay_near(c):
        recv(c, 2)
        rc(c, 6, X.at[2, rows(c), :], ahead).start()
        rc(c, 4, X.at[2, rows(c), :], partner).start()
        recv(c, 3)
        rc(c, 5, X.at[3, rows(c), :], partner).start()

    def relay_far(c):
        recv(c, 6)
        rc(c, 7, X.at[6, rows(c), :], partner).start()

    def recv_partner(c):
        for k in (1, 4, 5, 7):
            recv(c, k)

    send_own(0)
    send_own(1)

    for cp in small:
        cp.wait()
    lane = lax.broadcasted_iota(jnp.int32, (8, 128), 1)
    ln = jnp.broadcast_to(lens[...].astype(f32), (8, 128))
    cum = ln
    for k in (1, 2, 4, 8, 16, 32, 64):
        cum = cum + jnp.where(lane >= k, pltpu.roll(cum, k, 1), 0.0)
    starts = (cum - ln)[0:1, :]
    base = (a * (NC * QB)).astype(f32)
    sub = lax.broadcasted_iota(jnp.int32, (QB, QB), 0).astype(f32)
    for i in range(NC):
        pos = sub + (base + float(QB * i))
        cand = jnp.where(starts <= pos, jnp.broadcast_to(starts, (QB, QB)), 0.0)
        first = jnp.max(cand, axis=1, keepdims=True) - base
        FR[i] = jnp.broadcast_to(first, (QB, QB))
    for t, k in enumerate(kinds):
        for u in range(4):
            G[t, 0:1, u * 128:(u + 1) * 128] = gain[pl.ds(4 * k + u, 1), :]

    def kv_copy(j):
        return pltpu.make_async_remote_copy(
            src_ref=KV.at[j], dst_ref=PKV.at[j], send_sem=kvs_sem.at[j], recv_sem=kvr_sem.at[j],
            device_id=(nxt, p), device_id_type=MESH)

    def scale(j, ks, sq):
        for t in ks:
            xf = X[t, j * QB:(j + 1) * QB, :].astype(f32)
            XS[:, t * 512:(t + 1) * 512] = (xf * G[t, 0:1, :]).astype(bf16)
            x2 = xf * xf
            part = (x2[:, 0:128] + x2[:, 128:256]) + (x2[:, 256:384] + x2[:, 384:512])
            sq = part if sq is None else sq + part
        return sq

    def project(j, acc, sq):
        inv = lax.rsqrt(jnp.sum(sq, axis=1, keepdims=True) * (1.0 / 4096) + EPS)
        KV[j, :, :] = (acc[:, 512:768] * inv).astype(bf16)
        kv_copy(j).start()
        for h in range(4):
            Q[j, h * QB:(h + 1) * QB, :] = (acc[:, h * 128:(h + 1) * 128] * inv).astype(bf16)

    lane_f = lax.broadcasted_iota(jnp.int32, (QB, QB), 1).astype(f32)

    def update(i, parts, init):
        cs = LOG2E / HEAD ** 0.5
        masks = []
        for own, j in parts:
            off = float(QB * j - (0 if own else NC * QB))
            ok = (lane_f + off) >= FR[i]
            if own and j == i:
                ok = ok & (lane_f <= sub)
            masks.append(ok)
        for h in range(4):
            hr = slice(h * QB, (h + 1) * QB)
            q = Q[i, hr, :]
            ss = []
            for (own, j), ok in zip(parts, masks):
                kk = (KV if own else PKV)[j, :, 0:128]
                sc = lax.dot_general(q, kk, (((1,), (1,)), ((), ())), preferred_element_type=f32) * cs
                ss.append(jnp.where(ok, sc, NEG))
            mx = functools.reduce(jnp.maximum, ss)
            mx = jnp.broadcast_to(jnp.max(mx, axis=1, keepdims=True), (QB, QB))
            if not init:
                mo = M[i, hr, :]
                mx = jnp.maximum(mx, mo)
            ps = [jnp.exp2(sc - mx) for sc in ss]
            tot = functools.reduce(jnp.add, ps)
            tot = jnp.broadcast_to(jnp.sum(tot, axis=1, keepdims=True), (QB, QB))
            o = None
            for (own, j), pp in zip(parts, ps):
                vv = (KV if own else PKV)[j, :, 128:256]
                d = jnp.dot(pp.astype(bf16), vv, preferred_element_type=f32)
                o = d if o is None else o + d
            if not init:
                al = jnp.exp2(mo - mx)
                tot = tot + al * L[i, hr, :]
                o = o + al * ACC[i, hr, :]
            M[i, hr, :] = mx
            L[i, hr, :] = tot
            ACC[i, hr, :] = o

    def attend(j):
        for i in range(NC - 1, j + 1, -1):
            update(i, [(True, j)], False)
        if j + 1 < NC:
            kv_copy(j + 1).wait_recv()
            update(j + 1, [(True, j), (False, j + 1)], False)
        update(j, [(True, j)] + [(False, k) for k in range(j + 1, NC)], True)

    relay_near(0)
    send_own(2)
    relay_near(1)
    send_own(3)
    own_copy.wait()
    for t, k in enumerate(kinds):
        r = pl.ds(pl.multiple_of(k * 512, 512), 512)
        d = pl.ds(t * 512, 512)
        pltpu.make_async_copy(wq.at[r, :], W.at[d, pl.ds(0, 512)], w_sem.at[t, 0]).wait()
        pltpu.make_async_copy(wk.at[r, :], W.at[d, pl.ds(512, 128)], w_sem.at[t, 1]).wait()
        pltpu.make_async_copy(wv.at[r, :], W.at[d, pl.ds(640, 128)], w_sem.at[t, 2]).wait()

    for c in range(NC - 1):
        j = NC - 1 - c
        relay_far(c)
        recv_partner(c)
        sq = scale(j, range(8), None)
        acc = jnp.dot(XS[...], W[...], preferred_element_type=f32)
        project(j, acc, sq)
        if c + 2 < NC:
            relay_near(c + 2)
        attend(j)

    c = NC - 1
    for k in (1, 4, 5):
        recv(c, k)
    sq = scale(0, range(6), None)
    PART[...] = jnp.dot(XS[:, :3072], W[:3072, :], preferred_element_type=f32)
    relay_far(c)
    sq = scale(0, (6,), sq)
    recv(c, 7)
    sq = scale(0, (7,), sq)
    acc = PART[...] + jnp.dot(XS[:, 3072:], W[3072:, :], preferred_element_type=f32)
    project(0, acc, sq)
    attend(0)
    kv_copy(0).wait_recv()
    update(0, [(False, 0)], False)

    eye = sub == lane_f
    tiles = []
    srow = lax.broadcasted_iota(jnp.int32, (8, 128), 0)
    for i in range(NC):
        tile = jnp.ones((8, 128), f32)
        for h in range(4):
            hr = slice(h * QB, (h + 1) * QB)
            v = (M[i, hr, :] + jnp.log2(L[i, hr, :])) * LN2
            row = jnp.sum(jnp.where(eye, v, 0.0), axis=0, keepdims=True)
            tile = jnp.where(srow == h, jnp.broadcast_to(row, (8, 128)), tile)
        tiles.append(tile)
    srv = [served[i] for i in range(NC)]
    for d in range(n_attn):
        t = jnp.where(srv[0] == d, tiles[0], 0.0)
        for i in range(1, NC):
            t = t + jnp.where(srv[i] == d, tiles[i], 0.0)
        SLOT[d] = t

    def lse_copy(dst, slot):
        return pltpu.make_async_remote_copy(
            src_ref=SLOT.at[dst], dst_ref=RECV.at[slot], send_sem=ls_sem.at[dst], recv_sem=lr_sem.at[slot],
            device_id=(dst, p), device_id_type=MESH)

    for d in peers:
        lse_copy(d, a).start()
    RECV[a] = SLOT[a]

    for i in range(NC):
        for h in range(4):
            hr = slice(h * QB, (h + 1) * QB)
            out[i * QB:(i + 1) * QB, h * 128:(h + 1) * 128] = (ACC[i, hr, :] / L[i, hr, :]).astype(bf16)

    for d in peers:
        lse_copy(d, d).wait_recv()
    cnt = jnp.zeros((4, 128), f32)
    res = [jnp.zeros((4, 128), f32) for _ in range(NC)]
    for d in range(n_attn):
        t = RECV[d]
        f = jnp.broadcast_to(t[4:5, :], (4, 128))
        for i in range(NC):
            res[i] = jnp.where((cnt == float(i)) & (f > 0.5), t[0:4, :], res[i])
        cnt = cnt + f
    for i in range(NC):
        lse_out[i] = res[i]

    for c in range(NC):
        for k in (1, 2, 3, 4, 5, 6, 7):
            rc(c, k, X.at[k, rows(c), :], partner).wait_send()
    for j in range(NC):
        kv_copy(j).wait_send()
    for d in peers:
        lse_copy(d, a).wait_send()


def shards(n_attn, nz, tokens, norm_gain, w_query, w_key, value_matrix, doc_lengths, block_server):
    hbm = pl.BlockSpec(memory_space=pltpu.HBM)
    vm = pl.BlockSpec(memory_space=pltpu.VMEM)
    bf16, f32 = jnp.bfloat16, jnp.float32
    dma = pltpu.SemaphoreType.DMA
    return pl.pallas_call(
        functools.partial(fused, n_attn, nz),
        out_shape=(jax.ShapeDtypeStruct((512, 512), bf16), jax.ShapeDtypeStruct((4, 4, 128), f32)),
        in_specs=[hbm] * 7,
        out_specs=(vm, vm),
        scratch_shapes=[
            pltpu.VMEM((32, 128), f32),
            pltpu.VMEM((1, 128), jnp.int32),
            pltpu.SMEM((4,), jnp.int32),
            pltpu.VMEM((8, 512, 512), bf16),
            pltpu.VMEM((4096, 768), bf16),
            pltpu.VMEM((QB, 4096), bf16),
            pltpu.VMEM((8, 1, 512), f32),
            pltpu.VMEM((NC, QB, 256), bf16),
            pltpu.VMEM((NC, QB, 256), bf16),
            pltpu.VMEM((NC, 4 * QB, 128), bf16),
            pltpu.VMEM((NC, QB, QB), f32),
            pltpu.VMEM((NC, 4 * QB, 128), f32),
            pltpu.VMEM((NC, 4 * QB, 128), f32),
            pltpu.VMEM((NC, 4 * QB, 128), f32),
            pltpu.VMEM((n_attn, 8, 128), f32),
            pltpu.VMEM((n_attn, 8, 128), f32),
            pltpu.VMEM((QB, 768), f32),
            dma(()), dma((3,)), dma((8, 3)), dma((NC, 8)), dma((NC, 8)), dma((NC,)), dma((NC,)),
            dma((n_attn,)), dma((n_attn,)),
        ],
        compiler_params=pltpu.CompilerParams(
            collective_id=0, has_side_effects=True, vmem_limit_bytes=67043328),
        name="fused_attention",
    )(tokens, norm_gain.reshape(32, 128), w_query, w_key, value_matrix,
      doc_lengths.reshape(1, 128), block_server)


def solution(mesh):
    n_attn = mesh.shape["attn"]
    nz = 8 if n_attn % 8 == 0 else n_attn
    return jax.shard_map(
        functools.partial(shards, n_attn, nz),
        mesh=mesh,
        in_specs=(
            P("attn", "proj"),
            P(),
            P(None, "proj"),
            P(None, "proj"),
            P(None, "proj"),
            P(),
            P("attn"),
        ),
        out_specs=(P("attn", "proj"), P("attn", "proj", None)),
        check_vma=False,
    )
```

```python
import functools
import jax
import jax.numpy as jnp
from jax import lax
from jax.experimental import pallas as pl
from jax.experimental.pallas import tpu as pltpu
from jax.sharding import PartitionSpec as P

HEAD = 128
QB = 128
NEG = -1e30
EPS = 1e-05
LOG2E = 1.4426950408889634
LN2 = 0.6931471805599453
MESH = pl.DeviceIdType.MESH
NC = 4


def fused(n_attn, nz, tok, gain_h, wq, wk, wv, lens_h, served_h, out, lse_out,
          gain, lens, served, TOK, X, W, SQ, PSQ, INV, KV, PKV, Q, FR, M, L, ACC, LT, SLOT, RECV, PART,
          in_sem, w_sem, s_sem, r_sem, kvs_sem, kvr_sem, ls_sem, lr_sem, hop_sem):
    f32 = jnp.float32
    bf16 = jnp.bfloat16
    a = lax.axis_index("attn")
    p = lax.axis_index("proj")
    core = lax.rem(p, 2)
    s = 1 - 2 * core
    mod8 = lambda v: lax.rem(v + 16, 8)
    partner = p + s
    ahead = mod8(p + 2 * s)
    behind = mod8(p - 2 * s)
    kinds = [p, partner, behind, ahead, mod8(p + 3 * s), mod8(p - s), mod8(p + 4), mod8(p + s + 4)]
    ny = n_attn // nz
    y = a // nz
    z = lax.rem(a, nz)
    at = lambda dy, dz: lax.rem(y + dy, ny) * nz + lax.rem(z + dz, nz)
    offs = [(dy, dz) for dy in range(ny) for dz in range(nz) if (dy, dz) != (0, 0)]
    offs.sort(key=lambda o: -(min(o[0], ny - o[0]) + min(o[1], nz - o[1])))
    peers = [at(dy, dz) for dy, dz in offs]
    zs = (at(0, 1), at(0, nz - 1))
    ys = (at(1, 0), at(ny - 1, 0))
    nxt = lax.rem(a + 1, n_attn)
    prv = lax.rem(a + n_attn - 1, n_attn)

    small = [pltpu.make_async_copy(src, dst, in_sem.at[i])
             for i, (src, dst) in enumerate(((tok, TOK), (gain_h, gain), (lens_h, lens), (served_h, served)))]
    for cp in small:
        cp.start()

    barrier = pltpu.get_barrier_semaphore()
    for d in (ahead, behind, partner):
        pl.semaphore_signal(barrier, inc=1, device_id=(a, d), device_id_type=MESH)
    for d in zs + ys + (nxt, prv):
        pl.semaphore_signal(barrier, inc=1, device_id=(d, p), device_id_type=MESH)

    def w_copies(t, k):
        r = pl.ds(pl.multiple_of(k * 512, 512), 512)
        d = pl.ds(t * 512, 512)
        return (pltpu.make_async_copy(wq.at[r, :], W.at[d, pl.ds(0, 512)], w_sem.at[t, 0]),
                pltpu.make_async_copy(wk.at[r, :], W.at[d, pl.ds(512, 128)], w_sem.at[t, 1]),
                pltpu.make_async_copy(wv.at[r, :], W.at[d, pl.ds(640, 128)], w_sem.at[t, 2]))

    for t, k in enumerate(kinds):
        for cp in w_copies(t, k):
            cp.start()
    for cp in small:
        cp.wait()

    lane = lax.broadcasted_iota(jnp.int32, (QB, QB), 1).astype(f32)
    sub = lax.broadcasted_iota(jnp.int32, (QB, QB), 0).astype(f32)
    eye = sub == lane

    g = jnp.concatenate([gain[pl.ds(4 * p + u, 1), :] for u in range(4)], axis=1)

    def scale_rows(n, carry):
        r = pl.ds(pl.multiple_of(n * 32, 32), 32)
        xf = TOK[r, :].astype(f32)
        X[0, r, :] = (xf * g).astype(bf16)
        x2 = xf * xf
        PSQ[r, :] = (x2[:, 0:128] + x2[:, 128:256]) + (x2[:, 256:384] + x2[:, 384:512])
        return carry

    lax.fori_loop(0, NC * QB // 32, scale_rows, 0)
    for j in range(NC):
        col = jnp.sum(PSQ[j * QB:(j + 1) * QB, :], axis=1, keepdims=True)
        SQ[0, j:j + 1, :] = jnp.sum(jnp.where(eye, col, 0.0), axis=0, keepdims=True)
        SQ[0, NC + j:NC + j + 1, :] = jnp.zeros((1, QB), f32)

    pl.semaphore_wait(barrier, 9)

    def hop_signal(k):
        for d in (zs if k < 3 else ys):
            pl.semaphore_signal(hop_sem.at[k], inc=1, device_id=(d, p), device_id_type=MESH)

    def hop(k):
        pl.semaphore_wait(hop_sem.at[k], 2)
        if k < 4:
            hop_signal(k + 1)

    hop_signal(0)

    def view(c, kind):
        if c == NC:
            return SQ.at[kind]
        return X.at[kind, pl.ds((NC - 1 - c) * QB, QB), :]

    def rc(c, kind, src_kind, dst_proj):
        return pltpu.make_async_remote_copy(
            src_ref=view(c, src_kind), dst_ref=view(c, kind),
            send_sem=s_sem.at[c, kind], recv_sem=r_sem.at[c, kind],
            device_id=(a, dst_proj), device_id_type=MESH)

    def send_own(c):
        rc(c, 2, 0, ahead).start()
        rc(c, 3, 0, behind).start()
        rc(c, 1, 0, partner).start()

    def recv(c, kind):
        rc(c, kind, kind, partner).wait_recv()

    def relay_near(c):
        recv(c, 2)
        rc(c, 6, 2, ahead).start()
        rc(c, 4, 2, partner).start()
        recv(c, 3)
        rc(c, 5, 3, partner).start()

    def relay_far(c):
        recv(c, 6)
        rc(c, 7, 6, partner).start()

    def recv_partner(c):
        for k in (1, 4, 5, 7):
            recv(c, k)

    send_own(NC)
    send_own(0)
    send_own(1)

    ln = jnp.broadcast_to(lens[...].astype(f32), (8, 128))
    cum = ln
    for k in (1, 2, 4, 8, 16, 32, 64):
        cum = cum + jnp.where(lane[0:8] >= k, pltpu.roll(cum, k, 1), 0.0)
    starts = jnp.sum(jnp.where(eye, (cum - ln)[0:1, :], 0.0), axis=1, keepdims=True)
    base = (a * (NC * QB)).astype(f32)
    for i in range(NC):
        pos = lane + (base + float(QB * i))
        first = jnp.max(jnp.where(starts <= pos, starts, 0.0), axis=0, keepdims=True)
        FR[i:i + 1, :] = first - base

    def kv_copy(j):
        return pltpu.make_async_remote_copy(
            src_ref=KV.at[j], dst_ref=PKV.at[j], send_sem=kvs_sem.at[j], recv_sem=kvr_sem.at[j],
            device_id=(nxt, p), device_id_type=MESH)

    def lhs(j, ks):
        return jnp.concatenate([X[t, j * QB:(j + 1) * QB, :] for t in ks], axis=1)

    def project(j, acc):
        inv = INV[j]
        KV[j, 0] = (acc[:, 512:640] * inv).astype(bf16)
        KV[j, 1] = jnp.transpose(acc[:, 640:768] * inv).astype(bf16)
        kv_copy(j).start()
        for h in range(4):
            Q[j, h * QB:(h + 1) * QB, :] = (acc[:, h * 128:(h + 1) * 128] * inv).astype(bf16)

    def update(i, parts, init):
        cs = LOG2E / HEAD ** 0.5
        n = len(parts)
        oks = []
        for own, j in parts:
            off = float(QB * j - (0 if own else NC * QB))
            ok = (sub + off) >= FR[i:i + 1, :]
            if own and j == i:
                ok = ok & (sub <= lane)
            oks.append(ok)
        bufs = [(KV if own else PKV).at[j] for own, j in parts]
        kk = jnp.concatenate([b[0] for b in bufs], axis=0)
        vv = jnp.concatenate([b[1] for b in bufs], axis=1)
        for hp in range(2):
            q = Q[i, hp * 256:(hp + 1) * 256, :]
            sc = lax.dot_general(kk, q, (((1,), (1,)), ((), ())), preferred_element_type=f32)
            halves, als = [], []
            for u in range(2):
                h = 2 * hp + u
                ss = [jnp.where(oks[t], sc[t * QB:(t + 1) * QB, u * 128:(u + 1) * 128] * cs, NEG) for t in range(n)]
                mx = jnp.max(functools.reduce(jnp.maximum, ss), axis=0, keepdims=True)
                if not init:
                    mo = M[i, h:h + 1, :]
                    mx = jnp.maximum(mx, mo)
                ps = [jnp.exp2(x - mx) for x in ss]
                tot = jnp.sum(functools.reduce(jnp.add, ps), axis=0, keepdims=True)
                if not init:
                    al = jnp.exp2(mo - mx)
                    als.append(al)
                    tot = tot + al * L[i, h:h + 1, :]
                M[i, h:h + 1, :] = mx
                L[i, h:h + 1, :] = tot
                halves.append(jnp.concatenate([x.astype(bf16) for x in ps], axis=0))
            o = jnp.dot(vv, jnp.concatenate(halves, axis=1), preferred_element_type=f32)
            cols = slice(hp * 256, (hp + 1) * 256)
            if not init:
                o = o + jnp.concatenate(als, axis=1) * ACC[i, :, cols]
            ACC[i, :, cols] = o

    def attend(j):
        for i in range(NC - 1, j + 1, -1):
            update(i, [(True, j)], False)
        if j + 1 < NC:
            kv_copy(j + 1).wait_recv()
            update(j + 1, [(True, j), (False, j + 1)], False)
        parts = [(True, j)] + [(False, k) for k in range(NC - 1, j, -1)]
        for t in range(0, len(parts), 2):
            update(j, parts[t:t + 2], t == 0)

    relay_near(NC)
    relay_near(0)
    send_own(2)
    hop(0)
    relay_far(NC)
    relay_near(1)
    send_own(3)
    hop(1)
    recv_partner(NC)
    tot = SQ[0]
    for t in range(1, 8):
        tot = tot + SQ[t]
    rows_inv = lax.rsqrt(tot * (1.0 / 4096) + EPS)
    for j in range(NC):
        INV[j] = jnp.broadcast_to(jnp.sum(jnp.where(eye, rows_inv[j:j + 1, :], 0.0), axis=1, keepdims=True), (QB, QB))
    for t, k in enumerate(kinds):
        for cp in w_copies(t, k):
            cp.wait()

    for c in range(NC - 1):
        j = NC - 1 - c
        relay_far(c)
        hop(c + 2)
        recv_partner(c)
        acc = jnp.dot(lhs(j, range(8)), W[...], preferred_element_type=f32)
        project(j, acc)
        if c + 2 < NC:
            relay_near(c + 2)
        attend(j)

    c = NC - 1
    for k in (1, 4, 5):
        recv(c, k)
    PART[...] = jnp.dot(lhs(0, range(6)), W[:3072, :], preferred_element_type=f32)
    relay_far(c)
    recv(c, 7)
    project(0, PART[...] + jnp.dot(lhs(0, (6, 7)), W[3072:, :], preferred_element_type=f32))
    attend(0)
    kv_copy(0).wait_recv()
    update(0, [(False, 0)], False)

    for i in range(NC):
        LT[i, 0:4, :] = (M[i] + jnp.log2(L[i])) * LN2
        LT[i, 4:8, :] = jnp.ones((4, 128), f32)
    tiles = [LT[i] for i in range(NC)]
    srv = [served[i] for i in range(NC)]
    for d in range(n_attn):
        t = jnp.where(srv[0] == d, tiles[0], 0.0)
        for i in range(1, NC):
            t = t + jnp.where(srv[i] == d, tiles[i], 0.0)
        SLOT[d] = t

    def lse_copy(dst, slot):
        return pltpu.make_async_remote_copy(
            src_ref=SLOT.at[dst], dst_ref=RECV.at[slot], send_sem=ls_sem.at[dst], recv_sem=lr_sem.at[slot],
            device_id=(dst, p), device_id_type=MESH)

    for d in peers:
        lse_copy(d, a).start()
    RECV[a] = SLOT[a]

    for i in range(NC):
        for h in range(4):
            o = ACC[i, :, h * 128:(h + 1) * 128] / L[i, h:h + 1, :]
            out[i * QB:(i + 1) * QB, h * 128:(h + 1) * 128] = jnp.transpose(o).astype(bf16)

    for d in peers:
        lse_copy(d, d).wait_recv()
    cnt = jnp.zeros((4, 128), f32)
    res = [jnp.zeros((4, 128), f32) for _ in range(NC)]
    for d in range(n_attn):
        t = RECV[d]
        f = jnp.broadcast_to(t[4:5, :], (4, 128))
        for i in range(NC):
            res[i] = jnp.where((cnt == float(i)) & (f > 0.5), t[0:4, :], res[i])
        cnt = cnt + f
    for i in range(NC):
        lse_out[i] = res[i]

    for c in range(NC + 1):
        for k in (1, 2, 3, 4, 5, 6, 7):
            rc(c, k, k, partner).wait_send()
    for j in range(NC):
        kv_copy(j).wait_send()
    for d in peers:
        lse_copy(d, a).wait_send()


def shards(n_attn, nz, tokens, norm_gain, w_query, w_key, value_matrix, doc_lengths, block_server):
    hbm = pl.BlockSpec(memory_space=pltpu.HBM)
    vm = pl.BlockSpec(memory_space=pltpu.VMEM)
    bf16, f32 = jnp.bfloat16, jnp.float32
    dma = pltpu.SemaphoreType.DMA
    return pl.pallas_call(
        functools.partial(fused, n_attn, nz),
        out_shape=(jax.ShapeDtypeStruct((512, 512), bf16), jax.ShapeDtypeStruct((4, 4, 128), f32)),
        in_specs=[hbm] * 7,
        out_specs=(vm, vm),
        scratch_shapes=[
            pltpu.VMEM((32, 128), f32),
            pltpu.VMEM((1, 128), jnp.int32),
            pltpu.SMEM((4,), jnp.int32),
            pltpu.VMEM((512, 512), bf16),
            pltpu.VMEM((8, 512, 512), bf16),
            pltpu.VMEM((4096, 768), bf16),
            pltpu.VMEM((8, 8, 128), f32),
            pltpu.VMEM((512, 128), f32),
            pltpu.VMEM((NC, QB, QB), f32),
            pltpu.VMEM((NC, 2, QB, 128), bf16),
            pltpu.VMEM((NC, 2, QB, 128), bf16),
            pltpu.VMEM((NC, 4 * QB, 128), bf16),
            pltpu.VMEM((8, QB), f32),
            pltpu.VMEM((NC, 4, 128), f32),
            pltpu.VMEM((NC, 4, 128), f32),
            pltpu.VMEM((NC, 128, 4 * QB), f32),
            pltpu.VMEM((NC, 8, 128), f32),
            pltpu.VMEM((n_attn, 8, 128), f32),
            pltpu.VMEM((n_attn, 8, 128), f32),
            pltpu.VMEM((QB, 768), f32),
            dma((4,)), dma((8, 3)), dma((NC + 1, 8)), dma((NC + 1, 8)), dma((NC,)), dma((NC,)),
            dma((n_attn,)), dma((n_attn,)), pltpu.SemaphoreType.REGULAR((5,)),
        ],
        compiler_params=pltpu.CompilerParams(
            collective_id=0, has_side_effects=True, vmem_limit_bytes=67043328),
        name="fused_attention",
    )(tokens, norm_gain.reshape(32, 128), w_query, w_key, value_matrix,
      doc_lengths.reshape(1, 128), block_server)


def solution(mesh):
    n_attn = mesh.shape["attn"]
    nz = 8 if n_attn % 8 == 0 else n_attn
    return jax.shard_map(
        functools.partial(shards, n_attn, nz),
        mesh=mesh,
        in_specs=(
            P("attn", "proj"),
            P(),
            P(None, "proj"),
            P(None, "proj"),
            P(None, "proj"),
            P(),
            P("attn"),
        ),
        out_specs=(P("attn", "proj"), P("attn", "proj", None)),
        check_vma=False,
    )
```

```python
import functools
import jax
import jax.numpy as jnp
from jax import lax
from jax.experimental import pallas as pl
from jax.experimental.pallas import tpu as pltpu
from jax.sharding import PartitionSpec as P

HEAD = 128
QB = 128
NEG = -1e30
EPS = 1e-05
LOG2E = 1.4426950408889634
LN2 = 0.6931471805599453
MESH = pl.DeviceIdType.MESH
NC = 4


def fused(n_attn, nz, tok, gain_h, wq, wk, wv, lens_h, served_h, out, lse_out,
          gain, lens, served, TOK, X, W, SQ, PSQ, INV, KV, PKV, Q, FR, M, L, ACC, LT, SLOT, RECV, PART, PB, AL,
          in_sem, w_sem, s_sem, r_sem, kvs_sem, kvr_sem, ls_sem, lr_sem, hop_sem):
    f32 = jnp.float32
    bf16 = jnp.bfloat16
    a = lax.axis_index("attn")
    p = lax.axis_index("proj")
    core = lax.rem(p, 2)
    s = 1 - 2 * core
    mod8 = lambda v: lax.rem(v + 16, 8)
    partner = p + s
    ahead = mod8(p + 2 * s)
    behind = mod8(p - 2 * s)
    kinds = [p, partner, behind, ahead, mod8(p + 3 * s), mod8(p - s), mod8(p + 4), mod8(p + s + 4)]
    ny = n_attn // nz
    y = a // nz
    z = lax.rem(a, nz)
    at = lambda dy, dz: lax.rem(y + dy, ny) * nz + lax.rem(z + dz, nz)
    offs = [(dy, dz) for dy in range(ny) for dz in range(nz) if (dy, dz) != (0, 0)]
    offs.sort(key=lambda o: -(min(o[0], ny - o[0]) + min(o[1], nz - o[1])))
    peers = [at(dy, dz) for dy, dz in offs]
    zs = (at(0, 1), at(0, nz - 1))
    ys = (at(1, 0), at(ny - 1, 0))
    nxt = lax.rem(a + 1, n_attn)
    prv = lax.rem(a + n_attn - 1, n_attn)

    small = [pltpu.make_async_copy(src, dst, in_sem.at[i])
             for i, (src, dst) in enumerate(((tok, TOK), (gain_h, gain), (lens_h, lens), (served_h, served)))]
    for cp in small:
        cp.start()

    barrier = pltpu.get_barrier_semaphore()
    for d in (ahead, behind, partner):
        pl.semaphore_signal(barrier, inc=1, device_id=(a, d), device_id_type=MESH)
    for d in zs + ys + (nxt, prv):
        pl.semaphore_signal(barrier, inc=1, device_id=(d, p), device_id_type=MESH)

    def w_copies(t, k):
        r = pl.ds(pl.multiple_of(k * 512, 512), 512)
        d = pl.ds(t * 512, 512)
        return (pltpu.make_async_copy(wq.at[r, :], W.at[d, pl.ds(0, 512)], w_sem.at[t, 0]),
                pltpu.make_async_copy(wk.at[r, :], W.at[d, pl.ds(512, 128)], w_sem.at[t, 1]),
                pltpu.make_async_copy(wv.at[r, :], W.at[d, pl.ds(640, 128)], w_sem.at[t, 2]))

    for t, k in enumerate(kinds):
        for cp in w_copies(t, k):
            cp.start()
    for cp in small:
        cp.wait()

    lane = lax.broadcasted_iota(jnp.int32, (QB, QB), 1).astype(f32)
    sub = lax.broadcasted_iota(jnp.int32, (QB, QB), 0).astype(f32)
    eye = sub == lane

    g = jnp.concatenate([gain[pl.ds(4 * p + u, 1), :] for u in range(4)], axis=1)

    def scale_rows(n, carry):
        r = pl.ds(pl.multiple_of(n * 32, 32), 32)
        xf = TOK[r, :].astype(f32)
        X[0, r, :] = (xf * g).astype(bf16)
        x2 = xf * xf
        PSQ[r, :] = (x2[:, 0:128] + x2[:, 128:256]) + (x2[:, 256:384] + x2[:, 384:512])
        return carry

    lax.fori_loop(0, NC * QB // 32, scale_rows, 0)
    for j in range(NC):
        col = jnp.sum(PSQ[j * QB:(j + 1) * QB, :], axis=1, keepdims=True)
        SQ[0, j:j + 1, :] = jnp.sum(jnp.where(eye, col, 0.0), axis=0, keepdims=True)
        SQ[0, NC + j:NC + j + 1, :] = jnp.zeros((1, QB), f32)

    pl.semaphore_wait(barrier, 9)

    def hop_signal(k):
        for d in (zs if k < 3 else ys):
            pl.semaphore_signal(hop_sem.at[k], inc=1, device_id=(d, p), device_id_type=MESH)

    def hop(k):
        pl.semaphore_wait(hop_sem.at[k], 2)
        if k < 4:
            hop_signal(k + 1)

    hop_signal(0)

    def view(c, kind):
        if c == NC:
            return SQ.at[kind]
        return X.at[kind, pl.ds((NC - 1 - c) * QB, QB), :]

    def rc(c, kind, src_kind, dst_proj):
        return pltpu.make_async_remote_copy(
            src_ref=view(c, src_kind), dst_ref=view(c, kind),
            send_sem=s_sem.at[c, kind], recv_sem=r_sem.at[c, kind],
            device_id=(a, dst_proj), device_id_type=MESH)

    def send_own(c):
        rc(c, 2, 0, ahead).start()
        rc(c, 3, 0, behind).start()
        rc(c, 1, 0, partner).start()

    def recv(c, kind):
        rc(c, kind, kind, partner).wait_recv()

    def relay_near(c):
        recv(c, 2)
        rc(c, 6, 2, ahead).start()
        rc(c, 4, 2, partner).start()
        recv(c, 3)
        rc(c, 5, 3, partner).start()

    def relay_far(c):
        recv(c, 6)
        rc(c, 7, 6, partner).start()

    def recv_partner(c):
        for k in (1, 4, 5, 7):
            recv(c, k)

    send_own(NC)
    send_own(0)
    send_own(1)

    ln = jnp.broadcast_to(lens[...].astype(f32), (8, 128))
    cum = ln
    for k in (1, 2, 4, 8, 16, 32, 64):
        cum = cum + jnp.where(lane[0:8] >= k, pltpu.roll(cum, k, 1), 0.0)
    starts = jnp.sum(jnp.where(eye, (cum - ln)[0:1, :], 0.0), axis=1, keepdims=True)
    base = (a * (NC * QB)).astype(f32)
    for i in range(NC):
        pos = lane + (base + float(QB * i))
        first = jnp.max(jnp.where(starts <= pos, starts, 0.0), axis=0, keepdims=True)
        FR[i:i + 1, :] = first - base

    def kv_copy(j):
        return pltpu.make_async_remote_copy(
            src_ref=KV.at[j], dst_ref=PKV.at[j], send_sem=kvs_sem.at[j], recv_sem=kvr_sem.at[j],
            device_id=(nxt, p), device_id_type=MESH)

    def lhs(j, ks):
        return jnp.concatenate([X[t, j * QB:(j + 1) * QB, :] for t in ks], axis=1)

    def project(j, acc):
        inv = INV[j]
        KV[j, 0] = (acc[:, 512:640] * inv).astype(bf16)
        KV[j, 1] = jnp.transpose(acc[:, 640:768] * inv).astype(bf16)
        kv_copy(j).start()
        for h in range(4):
            Q[j, h * QB:(h + 1) * QB, :] = (acc[:, h * 128:(h + 1) * 128] * inv).astype(bf16)

    def part_refs(parts):
        return [(KV if own else PKV).at[j] for own, j in parts]

    def apply(i, hp, parts, pp, al, init):
        vv = jnp.concatenate([b[1] for b in part_refs(parts)], axis=1)
        o = jnp.dot(vv, pp, preferred_element_type=f32)
        cols = slice(hp * 256, (hp + 1) * 256)
        if not init:
            o = o + al * ACC[i, :, cols]
        ACC[i, :, cols] = o

    later = []

    def update(i, parts, init, defer=False):
        cs = LOG2E / HEAD ** 0.5
        n = len(parts)
        oks = []
        for own, j in parts:
            off = float(QB * j - (0 if own else NC * QB))
            ok = (sub + off) >= FR[i:i + 1, :]
            if own and j == i:
                ok = ok & (sub <= lane)
            oks.append(ok)
        kk = jnp.concatenate([b[0] for b in part_refs(parts)], axis=0)
        for hp in range(2):
            q = Q[i, hp * 256:(hp + 1) * 256, :]
            sc = lax.dot_general(kk, q, (((1,), (1,)), ((), ())), preferred_element_type=f32)
            halves, als = [], []
            for u in range(2):
                h = 2 * hp + u
                ss = [jnp.where(oks[t], sc[t * QB:(t + 1) * QB, u * 128:(u + 1) * 128] * cs, NEG) for t in range(n)]
                mx = jnp.max(functools.reduce(jnp.maximum, ss), axis=0, keepdims=True)
                if not init:
                    mo = M[i, h:h + 1, :]
                    mx = jnp.maximum(mx, mo)
                ps = [jnp.exp2(x - mx) for x in ss]
                tot = jnp.sum(functools.reduce(jnp.add, ps), axis=0, keepdims=True)
                if not init:
                    al = jnp.exp2(mo - mx)
                    als.append(al)
                    tot = tot + al * L[i, h:h + 1, :]
                M[i, h:h + 1, :] = mx
                L[i, h:h + 1, :] = tot
                halves.append(jnp.concatenate([x.astype(bf16) for x in ps], axis=0))
            pp = jnp.concatenate(halves, axis=1)
            al = None if init else jnp.concatenate(als, axis=1)
            if defer:
                slot = len(later)
                PB[slot, 0:n * QB, :] = pp
                if not init:
                    AL[slot:slot + 1, :] = al
                later.append((i, hp, parts, slot, init))
            else:
                apply(i, hp, parts, pp, al, init)

    def attend(j):
        last = j == 0
        for i in range(NC - 1, j + 1, -1):
            update(i, [(True, j)], False, last)
        if j + 1 < NC:
            kv_copy(j + 1).wait_recv()
            update(j + 1, [(True, j), (False, j + 1)], False, last)
        parts = [(True, j)] + [(False, k) for k in range(NC - 1, j, -1)]
        for t in range(0, len(parts), 2):
            update(j, parts[t:t + 2], t == 0, last)

    def first_part(c):
        for k in (1, 4, 5):
            recv(c, k)
        PART[c] = jnp.dot(lhs(NC - 1 - c, range(6)), W[:3072, :], preferred_element_type=f32)

    def second_part(c):
        j = NC - 1 - c
        recv(c, 7)
        project(j, PART[c] + jnp.dot(lhs(j, (6, 7)), W[3072:, :], preferred_element_type=f32))

    relay_near(NC)
    relay_near(0)
    send_own(2)
    for t, k in enumerate(kinds):
        for cp in w_copies(t, k):
            cp.wait()
    first_part(0)
    relay_near(1)
    send_own(3)
    relay_far(NC)
    first_part(1)
    hop(0)
    relay_far(0)
    recv_partner(NC)
    tot = SQ[0]
    for t in range(1, 8):
        tot = tot + SQ[t]
    rows_inv = lax.rsqrt(tot * (1.0 / 4096) + EPS)
    for j in range(NC):
        INV[j] = jnp.broadcast_to(jnp.sum(jnp.where(eye, rows_inv[j:j + 1, :], 0.0), axis=1, keepdims=True), (QB, QB))
    hop(1)
    second_part(0)
    relay_near(2)
    attend(3)
    first_part(2)
    hop(2)
    relay_far(1)
    relay_near(3)
    second_part(1)
    hop(3)
    attend(2)
    relay_far(2)
    first_part(3)
    second_part(2)
    relay_far(3)
    hop(4)
    attend(1)
    second_part(3)
    attend(0)
    kv_copy(0).wait_recv()
    update(0, [(False, 0)], False, True)

    for i in range(NC):
        LT[i, 0:4, :] = (M[i] + jnp.log2(L[i])) * LN2
        LT[i, 4:8, :] = jnp.ones((4, 128), f32)
    tiles = [LT[i] for i in range(NC)]
    srv = [served[i] for i in range(NC)]
    for d in range(n_attn):
        t = jnp.where(srv[0] == d, tiles[0], 0.0)
        for i in range(1, NC):
            t = t + jnp.where(srv[i] == d, tiles[i], 0.0)
        SLOT[d] = t

    def lse_copy(dst, slot):
        return pltpu.make_async_remote_copy(
            src_ref=SLOT.at[dst], dst_ref=RECV.at[slot], send_sem=ls_sem.at[dst], recv_sem=lr_sem.at[slot],
            device_id=(dst, p), device_id_type=MESH)

    for d in peers:
        lse_copy(d, a).start()
    RECV[a] = SLOT[a]

    for i, hp, parts, slot, init in later:
        apply(i, hp, parts, PB[slot, 0:len(parts) * QB, :], None if init else AL[slot:slot + 1, :], init)

    for i in range(NC):
        for h in range(4):
            o = ACC[i, :, h * 128:(h + 1) * 128] / L[i, h:h + 1, :]
            out[i * QB:(i + 1) * QB, h * 128:(h + 1) * 128] = jnp.transpose(o).astype(bf16)

    for d in peers:
        lse_copy(d, d).wait_recv()
    cnt = jnp.zeros((4, 128), f32)
    res = [jnp.zeros((4, 128), f32) for _ in range(NC)]
    for d in range(n_attn):
        t = RECV[d]
        f = jnp.broadcast_to(t[4:5, :], (4, 128))
        for i in range(NC):
            res[i] = jnp.where((cnt == float(i)) & (f > 0.5), t[0:4, :], res[i])
        cnt = cnt + f
    for i in range(NC):
        lse_out[i] = res[i]

    for c in range(NC + 1):
        for k in (1, 2, 3, 4, 5, 6, 7):
            rc(c, k, k, partner).wait_send()
    for j in range(NC):
        kv_copy(j).wait_send()
    for d in peers:
        lse_copy(d, a).wait_send()


def shards(n_attn, nz, tokens, norm_gain, w_query, w_key, value_matrix, doc_lengths, block_server):
    hbm = pl.BlockSpec(memory_space=pl.ANY)
    vm = pl.BlockSpec(memory_space=pltpu.VMEM)
    bf16, f32 = jnp.bfloat16, jnp.float32
    dma = pltpu.SemaphoreType.DMA
    return pl.pallas_call(
        functools.partial(fused, n_attn, nz),
        out_shape=(jax.ShapeDtypeStruct((512, 512), bf16), jax.ShapeDtypeStruct((4, 4, 128), f32)),
        in_specs=[hbm] * 7,
        out_specs=(vm, vm),
        scratch_shapes=[
            pltpu.VMEM((32, 128), f32),
            pltpu.VMEM((1, 128), jnp.int32),
            pltpu.SMEM((4,), jnp.int32),
            pltpu.VMEM((512, 512), bf16),
            pltpu.VMEM((8, 512, 512), bf16),
            pltpu.VMEM((4096, 768), bf16),
            pltpu.VMEM((8, 8, 128), f32),
            pltpu.VMEM((512, 128), f32),
            pltpu.VMEM((NC, QB, QB), f32),
            pltpu.VMEM((NC, 2, QB, 128), bf16),
            pltpu.VMEM((NC, 2, QB, 128), bf16),
            pltpu.VMEM((NC, 4 * QB, 128), bf16),
            pltpu.VMEM((8, QB), f32),
            pltpu.VMEM((NC, 4, 128), f32),
            pltpu.VMEM((NC, 4, 128), f32),
            pltpu.VMEM((NC, 128, 4 * QB), f32),
            pltpu.VMEM((NC, 8, 128), f32),
            pltpu.VMEM((n_attn, 8, 128), f32),
            pltpu.VMEM((n_attn, 8, 128), f32),
            pltpu.VMEM((NC, QB, 768), f32),
            pltpu.VMEM((12, 2 * QB, 256), bf16),
            pltpu.VMEM((16, 256), f32),
            dma((4,)), dma((8, 3)), dma((NC + 1, 8)), dma((NC + 1, 8)), dma((NC,)), dma((NC,)),
            dma((n_attn,)), dma((n_attn,)), pltpu.SemaphoreType.REGULAR((5,)),
        ],
        compiler_params=pltpu.CompilerParams(
            collective_id=0, has_side_effects=True, vmem_limit_bytes=48 << 20),
        name="fused_attention",
    )(*[pltpu.with_memory_space_constraint(t, pltpu.HBM) for t in (
        tokens, norm_gain.reshape(32, 128), w_query, w_key, value_matrix,
        doc_lengths.reshape(1, 128), block_server)])


def solution(mesh):
    n_attn = mesh.shape["attn"]
    nz = 8 if n_attn % 8 == 0 else n_attn
    return jax.shard_map(
        functools.partial(shards, n_attn, nz),
        mesh=mesh,
        in_specs=(
            P("attn", "proj"),
            P(),
            P(None, "proj"),
            P(None, "proj"),
            P(None, "proj"),
            P(),
            P("attn"),
        ),
        out_specs=(P("attn", "proj"), P("attn", "proj", None)),
        check_vma=False,
    )
```

```python
import functools
import jax
import jax.numpy as jnp
from jax import lax
from jax.experimental import pallas as pl
from jax.experimental.pallas import tpu as pltpu
from jax.sharding import PartitionSpec as P

HEAD = 128
QB = 128
NEG = -1e30
EPS = 1e-05
LOG2E = 1.4426950408889634
LN2 = 0.6931471805599453
MESH = pl.DeviceIdType.MESH
NC = 4


def fused(n_attn, nz, tok, gain_h, wq, wk, wv, lens_h, served_h, out, lse_out,
          gain, lens, served, TOK, X, W, SQ, PSQ, INV, KV, PKV, Q, FR, M, L, LT, SLOT, RECV, PART, PB, AL,
          in_sem, w_sem, s_sem, r_sem, kvs_sem, kvr_sem, ls_sem, lr_sem, hop_sem):
    f32 = jnp.float32
    bf16 = jnp.bfloat16
    a = lax.axis_index("attn")
    p = lax.axis_index("proj")
    core = lax.rem(p, 2)
    s = 1 - 2 * core
    mod8 = lambda v: lax.rem(v + 16, 8)
    partner = p + s
    ahead = mod8(p + 2 * s)
    behind = mod8(p - 2 * s)
    kinds = [p, partner, behind, ahead, mod8(p + 3 * s), mod8(p - s), mod8(p + 4), mod8(p + s + 4)]
    ny = n_attn // nz
    y = a // nz
    z = lax.rem(a, nz)
    at = lambda dy, dz: lax.rem(y + dy, ny) * nz + lax.rem(z + dz, nz)
    offs = [(dy, dz) for dy in range(ny) for dz in range(nz) if (dy, dz) != (0, 0)]
    offs.sort(key=lambda o: -(min(o[0], ny - o[0]) + min(o[1], nz - o[1])))
    peers = [at(dy, dz) for dy, dz in offs]
    zs = (at(0, 1), at(0, nz - 1))
    ys = (at(1, 0), at(ny - 1, 0))
    nxt = lax.rem(a + 1, n_attn)
    prv = lax.rem(a + n_attn - 1, n_attn)

    blk = lambda j: pl.ds(j * QB, QB)
    small = [pltpu.make_async_copy(src, dst, in_sem.at[i])
             for i, (src, dst) in enumerate((
                 (gain_h, gain), (tok.at[blk(NC - 1), :], TOK.at[blk(NC - 1), :]),
                 (tok.at[pl.ds(0, (NC - 1) * QB), :], TOK.at[pl.ds(0, (NC - 1) * QB), :]),
                 (lens_h, lens), (served_h, served)))]
    for cp in small:
        cp.start()

    barrier = pltpu.get_barrier_semaphore()
    for d in (ahead, behind, partner):
        pl.semaphore_signal(barrier, inc=1, device_id=(a, d), device_id_type=MESH)
    for d in zs + ys + (nxt, prv):
        pl.semaphore_signal(barrier, inc=1, device_id=(d, p), device_id_type=MESH)

    def w_copies(t, k):
        r = pl.ds(pl.multiple_of(k * 512, 512), 512)
        d = pl.ds(t * 512, 512)
        return (pltpu.make_async_copy(wq.at[r, :], W.at[d, pl.ds(0, 512)], w_sem.at[t, 0]),
                pltpu.make_async_copy(wk.at[r, :], W.at[d, pl.ds(512, 128)], w_sem.at[t, 1]),
                pltpu.make_async_copy(wv.at[r, :], W.at[d, pl.ds(640, 128)], w_sem.at[t, 2]))

    for t, k in enumerate(kinds):
        for cp in w_copies(t, k):
            cp.start()

    lane = lax.broadcasted_iota(jnp.int32, (QB, QB), 1).astype(f32)
    sub = lax.broadcasted_iota(jnp.int32, (QB, QB), 0).astype(f32)
    eye = sub == lane

    small[0].wait()
    g = jnp.concatenate([gain[pl.ds(4 * p + u, 1), :] for u in range(4)], axis=1)

    def scale_rows(n, carry):
        r = pl.ds(pl.multiple_of(n * 32, 32), 32)
        xf = TOK[r, :].astype(f32)
        X[0, r, :] = (xf * g).astype(bf16)
        x2 = xf * xf
        PSQ[r, :] = (x2[:, 0:128] + x2[:, 128:256]) + (x2[:, 256:384] + x2[:, 384:512])
        return carry

    per = QB // 32
    small[1].wait()
    lax.fori_loop((NC - 1) * per, NC * per, scale_rows, 0)
    pl.semaphore_wait(barrier, 9)

    def hop_signal(k):
        for d in (zs if k < 3 else ys):
            pl.semaphore_signal(hop_sem.at[k], inc=1, device_id=(d, p), device_id_type=MESH)

    def hop(k):
        pl.semaphore_wait(hop_sem.at[k], 2)
        if k < 4:
            hop_signal(k + 1)

    hop_signal(0)

    def view(c, kind):
        if c == NC:
            return SQ.at[kind]
        return X.at[kind, pl.ds((NC - 1 - c) * QB, QB), :]

    def rc(c, kind, src_kind, dst_proj):
        return pltpu.make_async_remote_copy(
            src_ref=view(c, src_kind), dst_ref=view(c, kind),
            send_sem=s_sem.at[c, kind], recv_sem=r_sem.at[c, kind],
            device_id=(a, dst_proj), device_id_type=MESH)

    def send_own(c):
        rc(c, 1, 0, partner).start()
        rc(c, 2, 0, ahead).start()
        rc(c, 3, 0, behind).start()

    def recv(c, kind):
        rc(c, kind, kind, partner).wait_recv()

    def fcopy(c, side):
        if c == NC:
            src, dst = SQ.at[2], SQ.at[6]
        else:
            r = pl.ds((NC - 1 - c) * QB + side * (QB // 2), QB // 2)
            src, dst = X.at[2 + side, r, :], X.at[6, r, :]
        k = 6 + 2 * side
        return pltpu.make_async_remote_copy(
            src_ref=src, dst_ref=dst, send_sem=s_sem.at[c, k], recv_sem=r_sem.at[c, k],
            device_id=(a, behind if side else ahead), device_id_type=MESH)

    def sides(c):
        return (0,) if c == NC else (0, 1)

    def relay_near(c):
        recv(c, 2)
        recv(c, 3)
        rc(c, 4, 2, partner).start()
        rc(c, 5, 3, partner).start()

    def forward(c):
        for t in sides(c):
            fcopy(c, t).start()

    def relay_far(c):
        for t in sides(c):
            fcopy(c, t).wait_recv()
        rc(c, 7, 6, partner).start()

    def recv_partner(c):
        for k in (1, 4, 5, 7):
            recv(c, k)

    send_own(0)
    small[2].wait()
    lax.fori_loop(0, (NC - 1) * per, scale_rows, 0)
    for j in range(NC):
        col = jnp.sum(PSQ[j * QB:(j + 1) * QB, :], axis=1, keepdims=True)
        SQ[0, j:j + 1, :] = jnp.sum(jnp.where(eye, col, 0.0), axis=0, keepdims=True)
        SQ[0, NC + j:NC + j + 1, :] = jnp.zeros((1, QB), f32)
    send_own(NC)

    @pl.when(core == 0)
    def _():
        send_own(1)

    small[3].wait()
    small[4].wait()
    ln = jnp.broadcast_to(lens[...].astype(f32), (8, 128))
    cum = ln
    for k in (1, 2, 4, 8, 16, 32, 64):
        cum = cum + jnp.where(lane[0:8] >= k, pltpu.roll(cum, k, 1), 0.0)
    starts = jnp.sum(jnp.where(eye, (cum - ln)[0:1, :], 0.0), axis=1, keepdims=True)
    base = (a * (NC * QB)).astype(f32)
    for i in range(NC):
        pos = lane + (base + float(QB * i))
        first = jnp.max(jnp.where(starts <= pos, starts, 0.0), axis=0, keepdims=True)
        FR[i:i + 1, :] = first - base

    def kv_copy(j):
        return pltpu.make_async_remote_copy(
            src_ref=KV.at[j], dst_ref=PKV.at[j], send_sem=kvs_sem.at[j], recv_sem=kvr_sem.at[j],
            device_id=(nxt, p), device_id_type=MESH)

    def lhs(j, ks):
        return jnp.concatenate([X[t, j * QB:(j + 1) * QB, :] for t in ks], axis=1)

    def project_kv(j, acc):
        inv = INV[j]
        KV[j, 0] = (acc[:, 0:128] * inv).astype(bf16)
        KV[j, 1] = jnp.transpose(acc[:, 128:256] * inv).astype(bf16)
        kv_copy(j).start()

    def project_q(j, acc):
        inv = INV[j]
        for h in range(4):
            Q[j, h * QB:(h + 1) * QB, :] = (acc[:, h * 128:(h + 1) * 128] * inv).astype(bf16)

    def part_refs(parts):
        return [(KV if own else PKV).at[j] for own, j in parts]

    later = []

    def update(i, parts, init):
        cs = LOG2E / HEAD ** 0.5
        n = len(parts)
        oks = []
        for own, j in parts:
            off = float(QB * j - (0 if own else NC * QB))
            ok = (sub + off) >= FR[i:i + 1, :]
            if own and j == i:
                ok = ok & (sub <= lane)
            oks.append(ok)
        kk = jnp.concatenate([b[0] for b in part_refs(parts)], axis=0)
        for hp in range(2):
            q = Q[i, hp * 256:(hp + 1) * 256, :]
            sc = lax.dot_general(kk, q, (((1,), (1,)), ((), ())), preferred_element_type=f32)
            halves, als = [], []
            for u in range(2):
                h = 2 * hp + u
                ss = [jnp.where(oks[t], sc[t * QB:(t + 1) * QB, u * 128:(u + 1) * 128] * cs, NEG) for t in range(n)]
                mx = jnp.max(functools.reduce(jnp.maximum, ss), axis=0, keepdims=True)
                if not init:
                    mo = M[i, h:h + 1, :]
                    mx = jnp.maximum(mx, mo)
                ps = [jnp.exp2(x - mx) for x in ss]
                tot = jnp.sum(functools.reduce(jnp.add, ps), axis=0, keepdims=True)
                if not init:
                    al = jnp.exp2(mo - mx)
                    als.append(al)
                    tot = tot + al * L[i, h:h + 1, :]
                M[i, h:h + 1, :] = mx
                L[i, h:h + 1, :] = tot
                halves.append(jnp.concatenate([x.astype(bf16) for x in ps], axis=0))
            pp = jnp.concatenate(halves, axis=1)
            al = None if init else jnp.concatenate(als, axis=1)
            slot = len(later)
            PB[slot, 0:n * QB, :] = pp
            if not init:
                AL[slot:slot + 1, :] = al
            later.append((i, hp, parts, slot, init))

    def attend_old(j):
        for i in range(NC - 1, j + 1, -1):
            update(i, [(True, j)], False)
        if j + 1 < NC:
            kv_copy(j + 1).wait_recv()
            update(j + 1, [(True, j), (False, j + 1)], False)

    def attend_new(j):
        parts = [(True, j)] + [(False, k) for k in range(NC - 1, j, -1)]
        for t in range(0, len(parts), 2):
            update(j, parts[t:t + 2], t == 0)

    def first_part(c):
        for k in (1, 4, 5):
            recv(c, k)
        PART[c] = jnp.dot(lhs(NC - 1 - c, range(6)), W[:3072, :], preferred_element_type=f32)

    def second_part(c):
        j = NC - 1 - c
        recv(c, 7)
        x = lhs(j, (6, 7))
        project_kv(j, PART[c, :, 512:768] + jnp.dot(x, W[3072:, 512:768], preferred_element_type=f32))
        project_q(j, PART[c, :, 0:512] + jnp.dot(x, W[3072:, 0:512], preferred_element_type=f32))

    relay_near(0)

    @pl.when(core == 1)
    def _():
        send_own(1)

    relay_near(NC)
    forward(NC)
    forward(0)
    send_own(2)
    for t, k in enumerate(kinds):
        for cp in w_copies(t, k):
            cp.wait()
    relay_near(1)
    first_part(0)
    relay_far(NC)
    relay_far(0)
    forward(1)
    send_own(3)
    first_part(1)
    recv_partner(NC)
    tot = SQ[0]
    for t in range(1, 8):
        tot = tot + SQ[t]
    rows_inv = lax.rsqrt(tot * (1.0 / 4096) + EPS)
    for j in range(NC):
        INV[j] = jnp.broadcast_to(jnp.sum(jnp.where(eye, rows_inv[j:j + 1, :], 0.0), axis=1, keepdims=True), (QB, QB))
    second_part(0)
    attend_new(3)
    hop(0)
    relay_near(2)
    relay_far(1)
    forward(2)
    first_part(2)
    second_part(1)
    attend_old(2)
    attend_new(2)
    hop(1)
    relay_near(3)
    forward(3)
    relay_far(2)
    first_part(3)
    hop(2)
    second_part(2)
    relay_far(3)
    attend_old(1)
    hop(3)
    second_part(3)
    attend_new(1)
    attend_old(0)
    attend_new(0)
    hop(4)
    kv_copy(0).wait_recv()
    update(0, [(False, 0)], False)

    for i in range(NC):
        LT[i, 0:4, :] = (M[i] + jnp.log2(L[i])) * LN2
        LT[i, 4:8, :] = jnp.ones((4, 128), f32)
    tiles = [LT[i] for i in range(NC)]
    srv = [served[i] for i in range(NC)]
    for d in range(n_attn):
        t = jnp.where(srv[0] == d, tiles[0], 0.0)
        for i in range(1, NC):
            t = t + jnp.where(srv[i] == d, tiles[i], 0.0)
        SLOT[d] = t

    def lse_copy(dst, slot):
        return pltpu.make_async_remote_copy(
            src_ref=SLOT.at[dst], dst_ref=RECV.at[slot], send_sem=ls_sem.at[dst], recv_sem=lr_sem.at[slot],
            device_id=(dst, p), device_id_type=MESH)

    for d in peers:
        lse_copy(d, a).start()
    RECV[a] = SLOT[a]

    for i in range(NC):
        for hp in range(2):
            o = None
            for _, _, parts, slot, init in [t for t in later if t[:2] == (i, hp)]:
                vv = jnp.concatenate([b[1] for b in part_refs(parts)], axis=1)
                d = jnp.dot(vv, PB[slot, 0:len(parts) * QB, :], preferred_element_type=f32)
                o = d if init else AL[slot:slot + 1, :] * o + d
            for u in range(2):
                h = 2 * hp + u
                res = o[:, u * 128:(u + 1) * 128] / L[i, h:h + 1, :]
                out[i * QB:(i + 1) * QB, h * 128:(h + 1) * 128] = jnp.transpose(res).astype(bf16)

    for d in peers:
        lse_copy(d, d).wait_recv()
    cnt = jnp.zeros((4, 128), f32)
    res = [jnp.zeros((4, 128), f32) for _ in range(NC)]
    for d in range(n_attn):
        t = RECV[d]
        f = jnp.broadcast_to(t[4:5, :], (4, 128))
        for i in range(NC):
            res[i] = jnp.where((cnt == float(i)) & (f > 0.5), t[0:4, :], res[i])
        cnt = cnt + f
    for i in range(NC):
        lse_out[i] = res[i]

    for c in range(NC + 1):
        for k in (1, 2, 3, 4, 5, 7):
            rc(c, k, k, partner).wait_send()
        for t in sides(c):
            fcopy(c, t).wait_send()
    for j in range(NC):
        kv_copy(j).wait_send()
    for d in peers:
        lse_copy(d, a).wait_send()


def shards(n_attn, nz, tokens, norm_gain, w_query, w_key, value_matrix, doc_lengths, block_server):
    hbm = pl.BlockSpec(memory_space=pl.ANY)
    vm = pl.BlockSpec(memory_space=pltpu.VMEM)
    bf16, f32 = jnp.bfloat16, jnp.float32
    dma = pltpu.SemaphoreType.DMA
    return pl.pallas_call(
        functools.partial(fused, n_attn, nz),
        out_shape=(jax.ShapeDtypeStruct((512, 512), bf16), jax.ShapeDtypeStruct((4, 4, 128), f32)),
        in_specs=[hbm] * 7,
        out_specs=(vm, vm),
        scratch_shapes=[
            pltpu.VMEM((32, 128), f32),
            pltpu.VMEM((1, 128), jnp.int32),
            pltpu.SMEM((4,), jnp.int32),
            pltpu.VMEM((512, 512), bf16),
            pltpu.VMEM((8, 512, 512), bf16),
            pltpu.VMEM((4096, 768), bf16),
            pltpu.VMEM((8, 8, 128), f32),
            pltpu.VMEM((512, 128), f32),
            pltpu.VMEM((NC, QB, QB), f32),
            pltpu.VMEM((NC, 2, QB, 128), bf16),
            pltpu.VMEM((NC, 2, QB, 128), bf16),
            pltpu.VMEM((NC, 4 * QB, 128), bf16),
            pltpu.VMEM((8, QB), f32),
            pltpu.VMEM((NC, 4, 128), f32),
            pltpu.VMEM((NC, 4, 128), f32),
            pltpu.VMEM((NC, 8, 128), f32),
            pltpu.VMEM((n_attn, 8, 128), f32),
            pltpu.VMEM((n_attn, 8, 128), f32),
            pltpu.VMEM((NC, QB, 768), f32),
            pltpu.VMEM((26, 2 * QB, 256), bf16),
            pltpu.VMEM((32, 256), f32),
            dma((5,)), dma((8, 3)), dma((NC + 1, 9)), dma((NC + 1, 9)), dma((NC,)), dma((NC,)),
            dma((n_attn,)), dma((n_attn,)), pltpu.SemaphoreType.REGULAR((5,)),
        ],
        compiler_params=pltpu.CompilerParams(
            collective_id=0, has_side_effects=True, vmem_limit_bytes=48 << 20),
        name="fused_attention",
    )(*[pltpu.with_memory_space_constraint(t, pltpu.HBM) for t in (
        tokens, norm_gain.reshape(32, 128), w_query, w_key, value_matrix,
        doc_lengths.reshape(1, 128), block_server)])


def solution(mesh):
    n_attn = mesh.shape["attn"]
    nz = 8 if n_attn % 8 == 0 else n_attn
    return jax.shard_map(
        functools.partial(shards, n_attn, nz),
        mesh=mesh,
        in_specs=(
            P("attn", "proj"),
            P(),
            P(None, "proj"),
            P(None, "proj"),
            P(None, "proj"),
            P(),
            P("attn"),
        ),
        out_specs=(P("attn", "proj"), P("attn", "proj", None)),
        check_vma=False,
    )
```

```python
import functools
import jax
import jax.numpy as jnp
from jax import lax
from jax.experimental import pallas as pl
from jax.experimental.pallas import tpu as pltpu
from jax.sharding import PartitionSpec as P

HEAD = 128
QB = 128
NEG = -1e30
EPS = 1e-05
LOG2E = 1.4426950408889634
LN2 = 0.6931471805599453
MESH = pl.DeviceIdType.MESH
NC = 4
PIECES = 4


def fused(n_attn, nz, tok, gain_h, wq, wk, wv, lens_h, served_h, out, lse_out,
          gain, lens, served, TOK, X, W, SQ, PSQ, INV, KV, PKV, Q, FR, M, L, LT, SLOT, RECV, PART, PB, AL,
          in_sem, w_sem, s_sem, r_sem, kvs_sem, kvr_sem, ls_sem, lr_sem, hop_sem):
    f32 = jnp.float32
    bf16 = jnp.bfloat16
    a = lax.axis_index("attn")
    p = lax.axis_index("proj")
    core = lax.rem(p, 2)
    s = 1 - 2 * core
    mod8 = lambda v: lax.rem(v + 16, 8)
    partner = p + s
    ahead = mod8(p + 2 * s)
    behind = mod8(p - 2 * s)
    kinds = [p, partner, behind, ahead, mod8(p + 3 * s), mod8(p - s), mod8(p + 4), mod8(p + s + 4)]
    ny = n_attn // nz
    y = a // nz
    z = lax.rem(a, nz)
    at = lambda dy, dz: lax.rem(y + dy, ny) * nz + lax.rem(z + dz, nz)
    offs = [(dy, dz) for dy in range(ny) for dz in range(nz) if (dy, dz) != (0, 0)]
    offs.sort(key=lambda o: -(min(o[0], ny - o[0]) + min(o[1], nz - o[1])))
    peers = [at(dy, dz) for dy, dz in offs]
    zs = (at(0, 1), at(0, nz - 1))
    ys = (at(1, 0), at(ny - 1, 0))
    nxt = lax.rem(a + 1, n_attn)
    prv = lax.rem(a + n_attn - 1, n_attn)

    blk = lambda j: pl.ds(j * QB, QB)
    small = [pltpu.make_async_copy(src, dst, in_sem.at[i])
             for i, (src, dst) in enumerate((
                 (gain_h, gain), (tok.at[blk(NC - 1), :], TOK.at[blk(NC - 1), :]),
                 (tok.at[pl.ds(0, (NC - 1) * QB), :], TOK.at[pl.ds(0, (NC - 1) * QB), :]),
                 (lens_h, lens), (served_h, served)))]
    for cp in small:
        cp.start()

    barrier = pltpu.get_barrier_semaphore()
    for d in (ahead, behind, partner):
        pl.semaphore_signal(barrier, inc=1, device_id=(a, d), device_id_type=MESH)
    for d in zs + ys + (nxt, prv):
        pl.semaphore_signal(barrier, inc=1, device_id=(d, p), device_id_type=MESH)

    def w_copies(t, k):
        r = pl.ds(pl.multiple_of(k * 512, 512), 512)
        d = pl.ds(t * 512, 512)
        return (pltpu.make_async_copy(wq.at[r, :], W.at[d, pl.ds(0, 512)], w_sem.at[t, 0]),
                pltpu.make_async_copy(wk.at[r, :], W.at[d, pl.ds(512, 128)], w_sem.at[t, 1]),
                pltpu.make_async_copy(wv.at[r, :], W.at[d, pl.ds(640, 128)], w_sem.at[t, 2]))


    lane = lax.broadcasted_iota(jnp.int32, (QB, QB), 1).astype(f32)
    sub = lax.broadcasted_iota(jnp.int32, (QB, QB), 0).astype(f32)
    eye = sub == lane

    small[0].wait()
    g = jnp.concatenate([gain[pl.ds(4 * p + u, 1), :] for u in range(4)], axis=1)

    def scale_rows(n, carry):
        r = pl.ds(pl.multiple_of(n * 32, 32), 32)
        xf = TOK[r, :].astype(f32)
        X[0, r, :] = (xf * g).astype(bf16)
        x2 = xf * xf
        PSQ[r, :] = (x2[:, 0:128] + x2[:, 128:256]) + (x2[:, 256:384] + x2[:, 384:512])
        return carry

    per = QB // 32
    small[1].wait()
    lax.fori_loop((NC - 1) * per, NC * per, scale_rows, 0)
    pl.semaphore_wait(barrier, 9)

    def hop_signal(k):
        for d in (zs if k < 3 else ys):
            pl.semaphore_signal(hop_sem.at[k], inc=1, device_id=(d, p), device_id_type=MESH)

    def hop(k):
        pl.semaphore_wait(hop_sem.at[k], 2)
        if k < 4:
            hop_signal(k + 1)

    hop_signal(0)

    def view(c, kind):
        if c == NC:
            return SQ.at[kind]
        return X.at[kind, pl.ds((NC - 1 - c) * QB, QB), :]

    def rc(c, kind, src_kind, dst_proj):
        return pltpu.make_async_remote_copy(
            src_ref=view(c, src_kind), dst_ref=view(c, kind),
            send_sem=s_sem.at[c, kind], recv_sem=r_sem.at[c, kind],
            device_id=(a, dst_proj), device_id_type=MESH)

    def share(c, kind, src_kind):
        if c == NC:
            rc(c, kind, src_kind, partner).start()
            return
        step = QB // PIECES
        for t in range(PIECES):
            r = pl.ds((NC - 1 - c) * QB + t * step, step)
            pltpu.make_async_remote_copy(
                src_ref=X.at[src_kind, r, :], dst_ref=X.at[kind, r, :],
                send_sem=s_sem.at[c, kind], recv_sem=r_sem.at[c, kind],
                device_id=(a, partner), device_id_type=MESH).start()

    def half_copy(side, piece):
        r = pl.ds((side ^ piece) * (QB // 2), QB // 2)
        k = 2 + side if piece == 0 else 9 + side
        return pltpu.make_async_remote_copy(
            src_ref=X.at[0, r, :], dst_ref=X.at[2 + side, r, :],
            send_sem=s_sem.at[NC - 1, k], recv_sem=r_sem.at[NC - 1, k],
            device_id=(a, behind if side else ahead), device_id_type=MESH)

    def send_own(c):
        if c != 0:
            share(c, 1, 0)
        if c == NC - 1:
            for piece in range(2):
                for side in range(2):
                    half_copy(side, piece).start()
            return
        rc(c, 2, 0, ahead).start()
        rc(c, 3, 0, behind).start()
        if c == 0:
            share(c, 1, 0)

    def recv(c, kind):
        rc(c, kind, kind, partner).wait_recv()

    def fcopy(c, side):
        if c == NC:
            src, dst = SQ.at[2], SQ.at[6]
        else:
            r = pl.ds((NC - 1 - c) * QB + side * (QB // 2), QB // 2)
            src, dst = X.at[2 + side, r, :], X.at[6, r, :]
        k = 6 + 2 * side
        return pltpu.make_async_remote_copy(
            src_ref=src, dst_ref=dst, send_sem=s_sem.at[c, k], recv_sem=r_sem.at[c, k],
            device_id=(a, behind if side else ahead), device_id_type=MESH)

    def sides(c):
        return (0,) if c == NC else (0, 1)

    def relay_first(c):
        for side in range(2):
            half_copy(side, 0).wait_recv()
            fcopy(c, side).start()

    def relay_near(c):
        if c == NC - 1:
            half_copy(0, 1).wait_recv()
            half_copy(1, 1).wait_recv()
        else:
            recv(c, 2)
            recv(c, 3)
        share(c, 4, 2)
        share(c, 5, 3)

    def forward(c):
        for t in sides(c):
            fcopy(c, t).start()

    def relay_far(c):
        for t in sides(c):
            fcopy(c, t).wait_recv()
        share(c, 7, 6)

    def recv_partner(c):
        for k in (1, 4, 5, 7):
            recv(c, k)

    send_own(0)
    for t, k in enumerate(kinds):
        for cp in w_copies(t, k):
            cp.start()
    small[2].wait()
    lax.fori_loop(0, (NC - 1) * per, scale_rows, 0)
    for j in range(NC):
        col = jnp.sum(PSQ[j * QB:(j + 1) * QB, :], axis=1, keepdims=True)
        SQ[0, j:j + 1, :] = jnp.sum(jnp.where(eye, col, 0.0), axis=0, keepdims=True)
        SQ[0, NC + j:NC + j + 1, :] = jnp.zeros((1, QB), f32)
    send_own(NC)

    @pl.when(core == 0)
    def _():
        send_own(1)

    small[3].wait()
    small[4].wait()
    ln = jnp.broadcast_to(lens[...].astype(f32), (8, 128))
    cum = ln
    for k in (1, 2, 4, 8, 16, 32, 64):
        cum = cum + jnp.where(lane[0:8] >= k, pltpu.roll(cum, k, 1), 0.0)
    starts = jnp.sum(jnp.where(eye, (cum - ln)[0:1, :], 0.0), axis=1, keepdims=True)
    base = (a * (NC * QB)).astype(f32)
    for i in range(NC):
        pos = lane + (base + float(QB * i))
        first = jnp.max(jnp.where(starts <= pos, starts, 0.0), axis=0, keepdims=True)
        FR[i:i + 1, :] = first - base

    def kv_copy(j, t):
        return pltpu.make_async_remote_copy(
            src_ref=KV.at[j, t], dst_ref=PKV.at[j, t], send_sem=kvs_sem.at[j, t], recv_sem=kvr_sem.at[j, t],
            device_id=(nxt, p), device_id_type=MESH)

    def lhs(j, ks):
        return jnp.concatenate([X[t, j * QB:(j + 1) * QB, :] for t in ks], axis=1)

    def project_kv(j, acc):
        inv = INV[j]
        KV[j, 0] = (acc[:, 0:128] * inv).astype(bf16)
        kv_copy(j, 0).start()
        KV[j, 1] = jnp.transpose(acc[:, 128:256] * inv).astype(bf16)
        kv_copy(j, 1).start()

    def project_q(j, acc):
        inv = INV[j]
        for h in range(4):
            Q[j, h * QB:(h + 1) * QB, :] = (acc[:, h * 128:(h + 1) * 128] * inv).astype(bf16)

    def part_refs(parts):
        return [(KV if own else PKV).at[j] for own, j in parts]

    later = []

    def update(i, parts, init):
        cs = LOG2E / HEAD ** 0.5
        n = len(parts)
        oks = []
        for own, j in parts:
            off = float(QB * j - (0 if own else NC * QB))
            ok = (sub + off) >= FR[i:i + 1, :]
            if own and j == i:
                ok = ok & (sub <= lane)
            oks.append(ok)
        kk = jnp.concatenate([b[0] for b in part_refs(parts)], axis=0)
        for hp in range(2):
            q = Q[i, hp * 256:(hp + 1) * 256, :]
            sc = lax.dot_general(kk, q, (((1,), (1,)), ((), ())), preferred_element_type=f32)
            halves, als = [], []
            for u in range(2):
                h = 2 * hp + u
                ss = [jnp.where(oks[t], sc[t * QB:(t + 1) * QB, u * 128:(u + 1) * 128] * cs, NEG) for t in range(n)]
                mx = jnp.max(functools.reduce(jnp.maximum, ss), axis=0, keepdims=True)
                if not init:
                    mo = M[i, h:h + 1, :]
                    mx = jnp.maximum(mx, mo)
                ps = [jnp.exp2(x - mx) for x in ss]
                tot = jnp.sum(functools.reduce(jnp.add, ps), axis=0, keepdims=True)
                if not init:
                    al = jnp.exp2(mo - mx)
                    als.append(al)
                    tot = tot + al * L[i, h:h + 1, :]
                M[i, h:h + 1, :] = mx
                L[i, h:h + 1, :] = tot
                halves.append(jnp.concatenate([x.astype(bf16) for x in ps], axis=0))
            pp = jnp.concatenate(halves, axis=1)
            al = None if init else jnp.concatenate(als, axis=1)
            slot = len(later)
            PB[slot, 0:n * QB, :] = pp
            if not init:
                AL[slot:slot + 1, :] = al
            later.append((i, hp, parts, slot, init))

    def attend_old(j):
        for i in range(NC - 1, j + 1, -1):
            update(i, [(True, j)], False)
        if j + 1 < NC:
            kv_copy(j + 1, 0).wait_recv()
            update(j + 1, [(True, j), (False, j + 1)], False)

    def attend_new(j):
        parts = [(True, j)] + [(False, k) for k in range(NC - 1, j, -1)]
        for t in range(0, len(parts), 2):
            update(j, parts[t:t + 2], t == 0)

    def first_part(c):
        for k in (1, 4, 5):
            recv(c, k)
        PART[c] = jnp.dot(lhs(NC - 1 - c, range(6)), W[:3072, :], preferred_element_type=f32)

    def second_part(c):
        j = NC - 1 - c
        recv(c, 7)
        x = lhs(j, (6, 7))
        project_kv(j, PART[c, :, 512:768] + jnp.dot(x, W[3072:, 512:768], preferred_element_type=f32))
        project_q(j, PART[c, :, 0:512] + jnp.dot(x, W[3072:, 0:512], preferred_element_type=f32))

    relay_near(0)

    @pl.when(core == 1)
    def _():
        send_own(1)

    relay_near(NC)
    forward(NC)
    forward(0)
    send_own(2)
    for t, k in enumerate(kinds):
        for cp in w_copies(t, k):
            cp.wait()
    relay_near(1)
    first_part(0)
    relay_far(NC)
    relay_far(0)
    forward(1)
    send_own(3)
    first_part(1)
    recv_partner(NC)
    tot = SQ[0]
    for t in range(1, 8):
        tot = tot + SQ[t]
    rows_inv = lax.rsqrt(tot * (1.0 / 4096) + EPS)
    for j in range(NC):
        INV[j] = jnp.broadcast_to(jnp.sum(jnp.where(eye, rows_inv[j:j + 1, :], 0.0), axis=1, keepdims=True), (QB, QB))
    second_part(0)
    attend_new(3)
    hop(0)
    relay_near(2)
    relay_far(1)
    forward(2)
    first_part(2)
    relay_first(3)
    second_part(1)
    attend_old(2)
    attend_new(2)
    hop(1)
    relay_near(3)
    relay_far(2)
    first_part(3)
    hop(2)
    second_part(2)
    relay_far(3)
    attend_old(1)
    hop(3)
    second_part(3)
    attend_new(1)
    attend_old(0)
    attend_new(0)
    hop(4)
    kv_copy(0, 0).wait_recv()
    update(0, [(False, 0)], False)

    for i in range(NC):
        LT[i, 0:4, :] = (M[i] + jnp.log2(L[i])) * LN2
        LT[i, 4:8, :] = jnp.ones((4, 128), f32)
    tiles = [LT[i] for i in range(NC)]
    srv = [served[i] for i in range(NC)]
    for d in range(n_attn):
        t = jnp.where(srv[0] == d, tiles[0], 0.0)
        for i in range(1, NC):
            t = t + jnp.where(srv[i] == d, tiles[i], 0.0)
        SLOT[d] = t

    def lse_copy(dst, slot):
        return pltpu.make_async_remote_copy(
            src_ref=SLOT.at[dst], dst_ref=RECV.at[slot], send_sem=ls_sem.at[dst], recv_sem=lr_sem.at[slot],
            device_id=(dst, p), device_id_type=MESH)

    for d in peers:
        lse_copy(d, a).start()
    RECV[a] = SLOT[a]

    for j in range(NC):
        kv_copy(j, 1).wait_recv()
    for i in range(NC):
        for hp in range(2):
            o = None
            for _, _, parts, slot, init in [t for t in later if t[:2] == (i, hp)]:
                vv = jnp.concatenate([b[1] for b in part_refs(parts)], axis=1)
                d = jnp.dot(vv, PB[slot, 0:len(parts) * QB, :], preferred_element_type=f32)
                o = d if init else AL[slot:slot + 1, :] * o + d
            for u in range(2):
                h = 2 * hp + u
                res = o[:, u * 128:(u + 1) * 128] / L[i, h:h + 1, :]
                out[i * QB:(i + 1) * QB, h * 128:(h + 1) * 128] = jnp.transpose(res).astype(bf16)

    for d in peers:
        lse_copy(d, d).wait_recv()
    cnt = jnp.zeros((4, 128), f32)
    res = [jnp.zeros((4, 128), f32) for _ in range(NC)]
    for d in range(n_attn):
        t = RECV[d]
        f = jnp.broadcast_to(t[4:5, :], (4, 128))
        for i in range(NC):
            res[i] = jnp.where((cnt == float(i)) & (f > 0.5), t[0:4, :], res[i])
        cnt = cnt + f
    for i in range(NC):
        lse_out[i] = res[i]

    for c in range(NC + 1):
        for k in (1, 4, 5, 7) if c == NC - 1 else (1, 2, 3, 4, 5, 7):
            rc(c, k, k, partner).wait_send()
        for t in sides(c):
            fcopy(c, t).wait_send()
    for side in range(2):
        for piece in range(2):
            half_copy(side, piece).wait_send()
    for j in range(NC):
        for t in range(2):
            kv_copy(j, t).wait_send()
    for d in peers:
        lse_copy(d, a).wait_send()


def shards(n_attn, nz, tokens, norm_gain, w_query, w_key, value_matrix, doc_lengths, block_server):
    hbm = pl.BlockSpec(memory_space=pl.ANY)
    vm = pl.BlockSpec(memory_space=pltpu.VMEM)
    bf16, f32 = jnp.bfloat16, jnp.float32
    dma = pltpu.SemaphoreType.DMA
    return pl.pallas_call(
        functools.partial(fused, n_attn, nz),
        out_shape=(jax.ShapeDtypeStruct((512, 512), bf16), jax.ShapeDtypeStruct((4, 4, 128), f32)),
        in_specs=[hbm] * 7,
        out_specs=(vm, vm),
        scratch_shapes=[
            pltpu.VMEM((32, 128), f32),
            pltpu.VMEM((1, 128), jnp.int32),
            pltpu.SMEM((4,), jnp.int32),
            pltpu.VMEM((512, 512), bf16),
            pltpu.VMEM((8, 512, 512), bf16),
            pltpu.VMEM((4096, 768), bf16),
            pltpu.VMEM((8, 8, 128), f32),
            pltpu.VMEM((512, 128), f32),
            pltpu.VMEM((NC, QB, QB), f32),
            pltpu.VMEM((NC, 2, QB, 128), bf16),
            pltpu.VMEM((NC, 2, QB, 128), bf16),
            pltpu.VMEM((NC, 4 * QB, 128), bf16),
            pltpu.VMEM((8, QB), f32),
            pltpu.VMEM((NC, 4, 128), f32),
            pltpu.VMEM((NC, 4, 128), f32),
            pltpu.VMEM((NC, 8, 128), f32),
            pltpu.VMEM((n_attn, 8, 128), f32),
            pltpu.VMEM((n_attn, 8, 128), f32),
            pltpu.VMEM((NC, QB, 768), f32),
            pltpu.VMEM((26, 2 * QB, 256), bf16),
            pltpu.VMEM((32, 256), f32),
            dma((5,)), dma((8, 3)), dma((NC + 1, 11)), dma((NC + 1, 11)), dma((NC, 2)), dma((NC, 2)),
            dma((n_attn,)), dma((n_attn,)), pltpu.SemaphoreType.REGULAR((5,)),
        ],
        compiler_params=pltpu.CompilerParams(
            collective_id=0, has_side_effects=True, vmem_limit_bytes=48 << 20),
        name="fused_attention",
    )(*[pltpu.with_memory_space_constraint(t, pltpu.HBM) for t in (
        tokens, norm_gain.reshape(32, 128), w_query, w_key, value_matrix,
        doc_lengths.reshape(1, 128), block_server)])


def solution(mesh):
    n_attn = mesh.shape["attn"]
    nz = 8 if n_attn % 8 == 0 else n_attn
    return jax.shard_map(
        functools.partial(shards, n_attn, nz),
        mesh=mesh,
        in_specs=(
            P("attn", "proj"),
            P(),
            P(None, "proj"),
            P(None, "proj"),
            P(None, "proj"),
            P(),
            P("attn"),
        ),
        out_specs=(P("attn", "proj"), P("attn", "proj", None)),
        check_vma=False,
    )
```

```python
import functools
import jax
import jax.numpy as jnp
from jax import lax
from jax.experimental import pallas as pl
from jax.experimental.pallas import tpu as pltpu
from jax.sharding import PartitionSpec as P

HEAD = 128
QB = 128
NEG = -1e30
EPS = 1e-05
LOG2E = 1.4426950408889634
LN2 = 0.6931471805599453
MESH = pl.DeviceIdType.MESH
NC = 4
PIECES = 4


def fused(n_attn, nz, tok, gain_h, wq, wk, wv, lens_h, served_h, out, lse_out,
          gain, lens, served, TOK, X, W, SQ, PSQ, INV, KV, PKV, Q, FR, M, L, LT, SLOT, RECV, PART, PB, AL,
          in_sem, w_sem, s_sem, r_sem, kvs_sem, kvr_sem, ls_sem, lr_sem, hop_sem):
    f32 = jnp.float32
    bf16 = jnp.bfloat16
    a = lax.axis_index("attn")
    p = lax.axis_index("proj")
    core = lax.rem(p, 2)
    s = 1 - 2 * core
    mod8 = lambda v: lax.rem(v + 16, 8)
    partner = p + s
    ahead = mod8(p + 2 * s)
    behind = mod8(p - 2 * s)
    kinds = [p, partner, behind, ahead, mod8(p + 3 * s), mod8(p - s), mod8(p + 4), mod8(p + s + 4)]
    ny = n_attn // nz
    y = a // nz
    z = lax.rem(a, nz)
    at = lambda dy, dz: lax.rem(y + dy, ny) * nz + lax.rem(z + dz, nz)
    offs = [(dy, dz) for dy in range(ny) for dz in range(nz) if (dy, dz) != (0, 0)]
    offs.sort(key=lambda o: -(min(o[0], ny - o[0]) + min(o[1], nz - o[1])))
    peers = [at(dy, dz) for dy, dz in offs]
    zs = (at(0, 1), at(0, nz - 1))
    ys = (at(1, 0), at(ny - 1, 0))
    nxt = lax.rem(a + 1, n_attn)
    prv = lax.rem(a + n_attn - 1, n_attn)

    blk = lambda j: pl.ds(j * QB, QB)
    small = [pltpu.make_async_copy(src, dst, in_sem.at[i])
             for i, (src, dst) in enumerate((
                 (gain_h, gain), (tok.at[blk(NC - 1), :], TOK.at[blk(NC - 1), :]),
                 (tok.at[pl.ds(0, (NC - 1) * QB), :], TOK.at[pl.ds(0, (NC - 1) * QB), :]),
                 (lens_h, lens), (served_h, served)))]
    for cp in small:
        cp.start()

    barrier = pltpu.get_barrier_semaphore()
    for d in (ahead, behind, partner):
        pl.semaphore_signal(barrier, inc=1, device_id=(a, d), device_id_type=MESH)
    for d in zs + ys + (nxt, prv):
        pl.semaphore_signal(barrier, inc=1, device_id=(d, p), device_id_type=MESH)

    def w_copies(t, k):
        r = pl.ds(pl.multiple_of(k * 512, 512), 512)
        d = pl.ds(t * 512, 512)
        return (pltpu.make_async_copy(wq.at[r, :], W.at[d, pl.ds(0, 512)], w_sem.at[t, 0]),
                pltpu.make_async_copy(wk.at[r, :], W.at[d, pl.ds(512, 128)], w_sem.at[t, 1]),
                pltpu.make_async_copy(wv.at[r, :], W.at[d, pl.ds(640, 128)], w_sem.at[t, 2]))


    lane = lax.broadcasted_iota(jnp.int32, (QB, QB), 1).astype(f32)
    sub = lax.broadcasted_iota(jnp.int32, (QB, QB), 0).astype(f32)
    eye = sub == lane

    small[0].wait()
    g = jnp.concatenate([gain[pl.ds(4 * p + u, 1), :] for u in range(4)], axis=1)

    def scale_rows(n, carry):
        r = pl.ds(pl.multiple_of(n * 32, 32), 32)
        xf = TOK[r, :].astype(f32)
        X[0, r, :] = (xf * g).astype(bf16)
        x2 = xf * xf
        PSQ[r, :] = (x2[:, 0:128] + x2[:, 128:256]) + (x2[:, 256:384] + x2[:, 384:512])
        return carry

    per = QB // 32
    small[1].wait()
    lax.fori_loop((NC - 1) * per, NC * per, scale_rows, 0)
    pl.semaphore_wait(barrier, 9)

    def hop_signal(k):
        for d in (zs if k < 3 else ys):
            pl.semaphore_signal(hop_sem.at[k], inc=1, device_id=(d, p), device_id_type=MESH)

    def hop(k):
        pl.semaphore_wait(hop_sem.at[k], 2)
        if k < 4:
            hop_signal(k + 1)

    hop_signal(0)

    def view(c, kind):
        if c == NC:
            return SQ.at[kind]
        return X.at[kind, pl.ds((NC - 1 - c) * QB, QB), :]

    def rc(c, kind, src_kind, dst_proj):
        return pltpu.make_async_remote_copy(
            src_ref=view(c, src_kind), dst_ref=view(c, kind),
            send_sem=s_sem.at[c, kind], recv_sem=r_sem.at[c, kind],
            device_id=(a, dst_proj), device_id_type=MESH)

    def share(c, kind, src_kind):
        if c == NC:
            rc(c, kind, src_kind, partner).start()
            return
        step = QB // PIECES
        for t in range(PIECES):
            r = pl.ds((NC - 1 - c) * QB + t * step, step)
            pltpu.make_async_remote_copy(
                src_ref=X.at[src_kind, r, :], dst_ref=X.at[kind, r, :],
                send_sem=s_sem.at[c, kind], recv_sem=r_sem.at[c, kind],
                device_id=(a, partner), device_id_type=MESH).start()

    def half_copy(side, piece):
        r = pl.ds((side ^ piece) * (QB // 2), QB // 2)
        k = 2 + side if piece == 0 else 9 + side
        return pltpu.make_async_remote_copy(
            src_ref=X.at[0, r, :], dst_ref=X.at[2 + side, r, :],
            send_sem=s_sem.at[NC - 1, k], recv_sem=r_sem.at[NC - 1, k],
            device_id=(a, behind if side else ahead), device_id_type=MESH)

    def send_own(c):
        if c != 0:
            share(c, 1, 0)
        if c == NC - 1:
            for piece in range(2):
                for side in range(2):
                    half_copy(side, piece).start()
            return
        rc(c, 2, 0, ahead).start()
        rc(c, 3, 0, behind).start()
        if c == 0:
            share(c, 1, 0)

    def recv(c, kind):
        rc(c, kind, kind, partner).wait_recv()

    def fcopy(c, side):
        if c == NC:
            src, dst = SQ.at[2], SQ.at[6]
        else:
            r = pl.ds((NC - 1 - c) * QB + side * (QB // 2), QB // 2)
            src, dst = X.at[2 + side, r, :], X.at[6, r, :]
        k = 6 + 2 * side
        return pltpu.make_async_remote_copy(
            src_ref=src, dst_ref=dst, send_sem=s_sem.at[c, k], recv_sem=r_sem.at[c, k],
            device_id=(a, behind if side else ahead), device_id_type=MESH)

    def sides(c):
        return (0,) if c == NC else (0, 1)

    def relay_first(c):
        for side in range(2):
            half_copy(side, 0).wait_recv()
            fcopy(c, side).start()

    def relay_near(c):
        if c == NC - 1:
            half_copy(0, 1).wait_recv()
            half_copy(1, 1).wait_recv()
        else:
            recv(c, 2)
            recv(c, 3)
        share(c, 4, 2)
        share(c, 5, 3)

    def forward(c):
        for t in sides(c):
            fcopy(c, t).start()

    def relay_far(c):
        for t in sides(c):
            fcopy(c, t).wait_recv()
        share(c, 7, 6)

    def recv_partner(c):
        for k in (1, 4, 5, 7):
            recv(c, k)

    send_own(0)
    for t, k in enumerate(kinds):
        for cp in w_copies(t, k):
            cp.start()
    small[2].wait()
    lax.fori_loop(0, (NC - 1) * per, scale_rows, 0)
    for j in range(NC):
        col = jnp.sum(PSQ[j * QB:(j + 1) * QB, :], axis=1, keepdims=True)
        SQ[0, j:j + 1, :] = jnp.sum(jnp.where(eye, col, 0.0), axis=0, keepdims=True)
        SQ[0, NC + j:NC + j + 1, :] = jnp.zeros((1, QB), f32)
    send_own(NC)

    @pl.when(core == 0)
    def _():
        send_own(1)

    small[3].wait()
    small[4].wait()
    ln = jnp.broadcast_to(lens[...].astype(f32), (8, 128))
    cum = ln
    for k in (1, 2, 4, 8, 16, 32, 64):
        cum = cum + jnp.where(lane[0:8] >= k, pltpu.roll(cum, k, 1), 0.0)
    starts = jnp.sum(jnp.where(eye, (cum - ln)[0:1, :], 0.0), axis=1, keepdims=True)
    base = (a * (NC * QB)).astype(f32)
    for i in range(NC):
        pos = lane + (base + float(QB * i))
        first = jnp.max(jnp.where(starts <= pos, starts, 0.0), axis=0, keepdims=True)
        FR[i:i + 1, :] = first - base

    def kv_copy(j, t):
        return pltpu.make_async_remote_copy(
            src_ref=KV.at[j, t], dst_ref=PKV.at[j, t], send_sem=kvs_sem.at[j, t], recv_sem=kvr_sem.at[j, t],
            device_id=(nxt, p), device_id_type=MESH)

    def lhs(j, ks):
        return jnp.concatenate([X[t, j * QB:(j + 1) * QB, :] for t in ks], axis=1)

    def project_kv(j, acc):
        inv = INV[j]
        KV[j, 0] = (acc[:, 0:128] * inv).astype(bf16)
        kv_copy(j, 0).start()
        KV[j, 1] = jnp.transpose(acc[:, 128:256] * inv).astype(bf16)
        kv_copy(j, 1).start()

    def project_q(j, acc):
        inv = INV[j]
        for h in range(4):
            Q[j, h * QB:(h + 1) * QB, :] = (acc[:, h * 128:(h + 1) * 128] * inv).astype(bf16)

    def part_refs(parts):
        return [(KV if own else PKV).at[j] for own, j in parts]

    later = []

    def update(i, parts, init):
        cs = LOG2E / HEAD ** 0.5
        n = len(parts)
        oks = []
        for own, j in parts:
            off = float(QB * j - (0 if own else NC * QB))
            ok = (sub + off) >= FR[i:i + 1, :]
            if own and j == i:
                ok = ok & (sub <= lane)
            oks.append(ok)
        kk = jnp.concatenate([b[0] for b in part_refs(parts)], axis=0)
        for hp in range(2):
            q = Q[i, hp * 256:(hp + 1) * 256, :]
            sc = lax.dot_general(kk, q, (((1,), (1,)), ((), ())), preferred_element_type=f32)
            halves, als = [], []
            for u in range(2):
                h = 2 * hp + u
                ss = [jnp.where(oks[t], sc[t * QB:(t + 1) * QB, u * 128:(u + 1) * 128] * cs, NEG) for t in range(n)]
                mx = jnp.max(functools.reduce(jnp.maximum, ss), axis=0, keepdims=True)
                if not init:
                    mo = M[i, h:h + 1, :]
                    mx = jnp.maximum(mx, mo)
                ps = [jnp.exp2(x - mx) for x in ss]
                tot = jnp.sum(functools.reduce(jnp.add, ps), axis=0, keepdims=True)
                if not init:
                    al = jnp.exp2(mo - mx)
                    als.append(al)
                    tot = tot + al * L[i, h:h + 1, :]
                M[i, h:h + 1, :] = mx
                L[i, h:h + 1, :] = tot
                halves.append(jnp.concatenate([x.astype(bf16) for x in ps], axis=0))
            pp = jnp.concatenate(halves, axis=1)
            al = None if init else jnp.concatenate(als, axis=1)
            slot = len(later)
            PB[slot, 0:n * QB, :] = pp
            if not init:
                AL[slot:slot + 1, :] = al
            later.append((i, hp, parts, slot, init))

    def attend_old(j):
        for i in range(NC - 1, j + 1, -1):
            update(i, [(True, j)], False)
        if j + 1 < NC:
            kv_copy(j + 1, 0).wait_recv()
            update(j + 1, [(True, j), (False, j + 1)], False)

    def attend_new(j):
        parts = [(True, j)] + [(False, k) for k in range(NC - 1, j, -1)]
        for t in range(0, len(parts), 2):
            update(j, parts[t:t + 2], t == 0)

    def first_part(c):
        for k in (1, 4, 5):
            recv(c, k)
        PART[c] = jnp.dot(lhs(NC - 1 - c, range(6)), W[:3072, :], preferred_element_type=f32)

    def second_part(c):
        j = NC - 1 - c
        recv(c, 7)
        x = lhs(j, (6, 7))
        project_kv(j, PART[c, :, 512:768] + jnp.dot(x, W[3072:, 512:768], preferred_element_type=f32))
        project_q(j, PART[c, :, 0:512] + jnp.dot(x, W[3072:, 0:512], preferred_element_type=f32))

    relay_near(0)

    @pl.when(core == 1)
    def _():
        send_own(1)

    relay_near(NC)
    forward(NC)
    forward(0)
    send_own(2)
    for t, k in enumerate(kinds):
        for cp in w_copies(t, k):
            cp.wait()
    relay_near(1)
    first_part(0)
    relay_far(NC)
    relay_far(0)
    forward(1)
    send_own(3)
    first_part(1)
    recv_partner(NC)
    tot = SQ[0]
    for t in range(1, 8):
        tot = tot + SQ[t]
    rows_inv = lax.rsqrt(tot * (1.0 / 4096) + EPS)
    for j in range(NC):
        INV[j] = jnp.broadcast_to(jnp.sum(jnp.where(eye, rows_inv[j:j + 1, :], 0.0), axis=1, keepdims=True), (QB, QB))
    second_part(0)
    attend_new(3)
    hop(0)
    relay_near(2)
    relay_far(1)
    forward(2)
    first_part(2)
    second_part(1)
    relay_first(3)
    attend_old(2)
    attend_new(2)
    hop(1)
    relay_near(3)
    relay_far(2)
    first_part(3)
    hop(2)
    second_part(2)
    relay_far(3)
    attend_old(1)
    hop(3)
    second_part(3)
    attend_new(1)
    attend_old(0)
    attend_new(0)
    hop(4)
    kv_copy(0, 0).wait_recv()
    update(0, [(False, 0)], False)

    for i in range(NC):
        LT[i, 0:4, :] = (M[i] + jnp.log2(L[i])) * LN2
        LT[i, 4:8, :] = jnp.ones((4, 128), f32)
    tiles = [LT[i] for i in range(NC)]
    srv = [served[i] for i in range(NC)]
    for d in range(n_attn):
        t = jnp.where(srv[0] == d, tiles[0], 0.0)
        for i in range(1, NC):
            t = t + jnp.where(srv[i] == d, tiles[i], 0.0)
        SLOT[d] = t

    def lse_copy(dst, slot):
        return pltpu.make_async_remote_copy(
            src_ref=SLOT.at[dst], dst_ref=RECV.at[slot], send_sem=ls_sem.at[dst], recv_sem=lr_sem.at[slot],
            device_id=(dst, p), device_id_type=MESH)

    for d in peers:
        lse_copy(d, a).start()
    RECV[a] = SLOT[a]

    for j in range(NC):
        kv_copy(j, 1).wait_recv()
    for i in range(NC):
        for hp in range(2):
            o = None
            for _, _, parts, slot, init in [t for t in later if t[:2] == (i, hp)]:
                vv = jnp.concatenate([b[1] for b in part_refs(parts)], axis=1)
                d = jnp.dot(vv, PB[slot, 0:len(parts) * QB, :], preferred_element_type=f32)
                o = d if init else AL[slot:slot + 1, :] * o + d
            for u in range(2):
                h = 2 * hp + u
                res = o[:, u * 128:(u + 1) * 128] / L[i, h:h + 1, :]
                out[i * QB:(i + 1) * QB, h * 128:(h + 1) * 128] = jnp.transpose(res).astype(bf16)

    for d in peers:
        lse_copy(d, d).wait_recv()
    cnt = jnp.zeros((4, 128), f32)
    res = [jnp.zeros((4, 128), f32) for _ in range(NC)]
    for d in range(n_attn):
        t = RECV[d]
        f = jnp.broadcast_to(t[4:5, :], (4, 128))
        for i in range(NC):
            res[i] = jnp.where((cnt == float(i)) & (f > 0.5), t[0:4, :], res[i])
        cnt = cnt + f
    for i in range(NC):
        lse_out[i] = res[i]

    for c in range(NC + 1):
        for k in (1, 4, 5, 7) if c == NC - 1 else (1, 2, 3, 4, 5, 7):
            rc(c, k, k, partner).wait_send()
        for t in sides(c):
            fcopy(c, t).wait_send()
    for side in range(2):
        for piece in range(2):
            half_copy(side, piece).wait_send()
    for j in range(NC):
        for t in range(2):
            kv_copy(j, t).wait_send()
    for d in peers:
        lse_copy(d, a).wait_send()


def store(a_ref, b_ref, a_out, b_out, sem):
    copies = [pltpu.make_async_copy(a_ref, a_out, sem.at[0]), pltpu.make_async_copy(b_ref, b_out, sem.at[1])]
    for cp in copies:
        cp.start()
    for cp in copies:
        cp.wait()


def shards(n_attn, nz, tokens, norm_gain, w_query, w_key, value_matrix, doc_lengths, block_server):
    hbm = pl.BlockSpec(memory_space=pl.ANY)
    vm = pl.BlockSpec(memory_space=pltpu.VMEM)
    bf16, f32 = jnp.bfloat16, jnp.float32
    dma = pltpu.SemaphoreType.DMA
    res = pl.pallas_call(
        functools.partial(fused, n_attn, nz),
        out_shape=(jax.ShapeDtypeStruct((512, 512), bf16), jax.ShapeDtypeStruct((4, 4, 128), f32)),
        in_specs=[hbm] * 7,
        out_specs=(vm, vm),
        scratch_shapes=[
            pltpu.VMEM((32, 128), f32),
            pltpu.VMEM((1, 128), jnp.int32),
            pltpu.SMEM((4,), jnp.int32),
            pltpu.VMEM((512, 512), bf16),
            pltpu.VMEM((8, 512, 512), bf16),
            pltpu.VMEM((4096, 768), bf16),
            pltpu.VMEM((8, 8, 128), f32),
            pltpu.VMEM((512, 128), f32),
            pltpu.VMEM((NC, QB, QB), f32),
            pltpu.VMEM((NC, 2, QB, 128), bf16),
            pltpu.VMEM((NC, 2, QB, 128), bf16),
            pltpu.VMEM((NC, 4 * QB, 128), bf16),
            pltpu.VMEM((8, QB), f32),
            pltpu.VMEM((NC, 4, 128), f32),
            pltpu.VMEM((NC, 4, 128), f32),
            pltpu.VMEM((NC, 8, 128), f32),
            pltpu.VMEM((n_attn, 8, 128), f32),
            pltpu.VMEM((n_attn, 8, 128), f32),
            pltpu.VMEM((NC, QB, 768), f32),
            pltpu.VMEM((26, 2 * QB, 256), bf16),
            pltpu.VMEM((32, 256), f32),
            dma((5,)), dma((8, 3)), dma((NC + 1, 11)), dma((NC + 1, 11)), dma((NC, 2)), dma((NC, 2)),
            dma((n_attn,)), dma((n_attn,)), pltpu.SemaphoreType.REGULAR((5,)),
        ],
        compiler_params=pltpu.CompilerParams(
            collective_id=0, has_side_effects=True, vmem_limit_bytes=48 << 20),
        name="fused_attention",
    )(*[pltpu.with_memory_space_constraint(t, pltpu.HBM) for t in (
        tokens, norm_gain.reshape(32, 128), w_query, w_key, value_matrix,
        doc_lengths.reshape(1, 128), block_server)])
    hbm = pl.BlockSpec(memory_space=pltpu.HBM)
    return pl.pallas_call(
        store,
        out_shape=(jax.ShapeDtypeStruct((512, 512), bf16), jax.ShapeDtypeStruct((4, 4, 128), f32)),
        in_specs=[vm, vm],
        out_specs=(hbm, hbm),
        scratch_shapes=[dma((2,))],
        compiler_params=pltpu.CompilerParams(vmem_limit_bytes=8 << 20),
        name="store_out",
    )(*res)


def solution(mesh):
    n_attn = mesh.shape["attn"]
    nz = 8 if n_attn % 8 == 0 else n_attn
    return jax.shard_map(
        functools.partial(shards, n_attn, nz),
        mesh=mesh,
        in_specs=(
            P("attn", "proj"),
            P(),
            P(None, "proj"),
            P(None, "proj"),
            P(None, "proj"),
            P(),
            P("attn"),
        ),
        out_specs=(P("attn", "proj"), P("attn", "proj", None)),
        check_vma=False,
    )
```
